32 devices in a mesh: parts: 2 (over y), tensor: 4 (over z), fsdp: 4 (over x, core).
Axes of the slice: x: 2, y: 2, z: 4, core: 2. Of those that a mesh axis runs over, the one named last changes fastest.
Arguments:
- tokens: bfloat16 [1024, 4096], P(('parts', 'fsdp'), 'tensor'), parts along dimension 0, may hold values from -6 to 6
- cotangent: bfloat16 [1024, 4096], P(('parts', 'fsdp'), 'tensor'), parts along dimension 0, may hold values from -6 to 6
- gate_values: bfloat16 [8, 160, 128, 128], P('fsdp', 'tensor'), may hold values from -0.1875 to 0.1875
- gate_rows: int32 [8, 160], P('fsdp', 'tensor'), may hold values from 0 to 31, as said below
- gate_scale: bfloat16 [8, 160], P('fsdp', 'tensor'), may hold values from 0.5 to 2
- up_values: bfloat16 [8, 160, 128, 128], P('fsdp', 'tensor'), may hold values from -0.1875 to 0.1875
- up_rows: int32 [8, 160], P('fsdp', 'tensor'), may hold values from 0 to 31, as said below
- up_scale: bfloat16 [8, 160], P('fsdp', 'tensor'), may hold values from 0.5 to 2
- down_values: bfloat16 [8, 160, 128, 128], P('fsdp', 'tensor'), may hold values from -0.078125 to 0.078125
- down_cols: int32 [8, 160], P('fsdp', 'tensor'), may hold values from 0 to 31, as said below
- down_scale: bfloat16 [8, 160], P('fsdp', 'tensor'), may hold values from 0.5 to 2
Outputs:
- layer_out: bfloat16 [1024, 4096], P(('parts', 'fsdp'), 'tensor'), parts along dimension 0
- grad_tokens: bfloat16 [1024, 4096], P(('parts', 'fsdp'), 'tensor'), parts along dimension 0
- grad_gate: bfloat16 [16, 160, 128, 128], P(('parts', 'fsdp'), 'tensor'), parts along dimension 0
- grad_up: bfloat16 [16, 160, 128, 128], P(('parts', 'fsdp'), 'tensor'), parts along dimension 0
- grad_down: bfloat16 [16, 160, 128, 128], P(('parts', 'fsdp'), 'tensor'), parts along dimension 0
The draws below stay inside these ranges and needn't reach their ends.
There are 2 independent parts, one for each index of `parts`. The reference program is written for one: setup_inputs(seed, part) draws one part's arguments, and reference() takes and returns one part's arrays. A program takes and returns all parts, laid end to end along the dimension named above; an argument that names none is the same for every part. Nothing has to cross between parts.
Inputs may be any that keep to these rules, and one draw needn't show every extreme that they name: `gate_rows`: the 8 entries of each column name distinct input blocks; some input blocks are named far more often than others. `up_rows`: the 8 entries of each column name distinct input blocks; some input blocks are named far more often than others. `down_cols`: the 8 entries of each column name distinct output blocks; some output blocks are named far more often than others.
All inputs are finite; a program needn't handle non-finite values.
Results may differ from the reference program's by a relative error of at most 0.023.
Values may be sent and summed in bfloat16 or wider, within the bound.
A program may use at most 192 MiB of HBM per device.

```python
import math
import jax
import jax.numpy as jnp
from jax import lax

D = 4096
FF = 20480
BLK = 128
K = 8
TOK_DEV = 128
TOKENS = 512
N_FSDP = 4


def pick_blocks(key):
    nblocks = D // BLK
    ncolumns = FF // BLK
    popular = jax.random.randint(jax.random.fold_in(key, 1), (nblocks,), 0, 1 << 20)
    noise = jax.random.randint(jax.random.fold_in(key, 2), (ncolumns, nblocks), 0, 1 << 20)
    column_ids = jnp.arange(ncolumns, dtype=jnp.int32)[:, None]
    block_ids = jnp.arange(nblocks, dtype=jnp.int32)[None, :]
    forced = (column_ids == 0) & (block_ids == 0) | (column_ids == 1) & (block_ids == nblocks - 1)
    scores = (noise + popular[None, :] + forced.astype(jnp.int32) * (1 << 22)) * nblocks + block_ids
    chosen = lax.top_k(scores, K)[1]
    return jnp.transpose(chosen).astype(jnp.int32)


def draw_gate_rows(key, part):
    return pick_blocks(jax.random.fold_in(key, 11))


def draw_up_rows(key, part):
    return pick_blocks(jax.random.fold_in(key, 12))


def draw_down_cols(key, part):
    return pick_blocks(jax.random.fold_in(key, 13))


def block_levels(own_key, shape, shards, smallest, largest):
    gain = 1.0
    for dim, shards_of in shards:
        steps = jax.random.uniform(jax.random.fold_in(jax.random.fold_in(own_key, 6), dim), (shards_of,), jnp.float32, smallest / len(shards), largest / len(shards))
        gain = gain * jnp.repeat(jnp.exp(steps), shape[dim] // shards_of).reshape((-1,) + (1,) * (len(shape) - 1 - dim))
    return gain


def normal_values(rng, dims, scale, limit, shards=(), kind=jnp.bfloat16):
    values = jax.random.normal(rng, dims, jnp.float32) * scale
    if len(shards) > 0:
        values = block_levels(rng, dims, shards, -0.22, 0.18) * values
    return jnp.clip(values, min=-limit, max=limit).astype(kind)


def setup_inputs(seed: int = 0, part: int = 0) -> dict:
    seeds = jax.random.split(jax.random.key(seed), 12)
    part_splits = jax.random.split(jax.random.fold_in(seeds[11], part), 12)
    tokens = normal_values(part_splits[0], (TOKENS, D), 1.0, 6.0, ((0, 4), (1, 4)))
    cotangent = normal_values(part_splits[1], (TOKENS, D), 0.5, 6.0, ((0, 4), (1, 4)))
    gate_values = normal_values(seeds[2], (K, FF // BLK, BLK, BLK), (K * BLK) ** -0.5, 0.1875, ((0, 4), (1, 4)))
    gate_rows = draw_gate_rows(jax.random.fold_in(seeds[11], 71), part)
    gate_scale = jnp.clip(jnp.exp(math.log(2.0) - 1.3862944 * jax.random.uniform(seeds[4], (K, FF // BLK), jnp.float32) ** block_levels(seeds[4], (K, FF // BLK), ((0, 4), (1, 4)), -0.2, 0.2)), 0.5, 2.0).astype(jnp.bfloat16)
    up_values = normal_values(seeds[5], (K, FF // BLK, BLK, BLK), (K * BLK) ** -0.5, 0.1875, ((0, 4), (1, 4)))
    up_rows = draw_up_rows(jax.random.fold_in(seeds[11], 71), part)
    up_scale = jnp.clip(jnp.exp(math.log(2.0) - 1.3862944 * jax.random.uniform(seeds[7], (K, FF // BLK), jnp.float32) ** block_levels(seeds[7], (K, FF // BLK), ((0, 4), (1, 4)), -0.2, 0.2)), 0.5, 2.0).astype(jnp.bfloat16)
    down_values = normal_values(seeds[8], (K, FF // BLK, BLK, BLK), (FF * K // (D // BLK)) ** -0.5, 0.078125, ((0, 4), (1, 4)))
    down_cols = draw_down_cols(jax.random.fold_in(seeds[11], 71), part)
    down_scale = jnp.clip(jnp.exp(math.log(2.0) - 1.3862944 * jax.random.uniform(seeds[10], (K, FF // BLK), jnp.float32) ** block_levels(seeds[10], (K, FF // BLK), ((0, 4), (1, 4)), -0.2, 0.2)), 0.5, 2.0).astype(jnp.bfloat16)
    return dict(tokens=tokens, cotangent=cotangent, gate_values=gate_values, gate_rows=gate_rows, gate_scale=gate_scale, up_values=up_values, up_rows=up_rows, up_scale=up_scale, down_values=down_values, down_cols=down_cols, down_scale=down_scale)


def weighted(selected, blocks, factors):
    products = jnp.einsum('tka,kab->tkb', selected, blocks.astype(jnp.float32))
    return jnp.sum(products * factors.astype(jnp.float32)[None, :, None], axis=1)


def rounded(values):
    return lax.optimization_barrier(values.astype(jnp.bfloat16)).astype(jnp.float32)


def group_sum(left, right, form, factors):
    left_groups = left.reshape((N_FSDP, TOK_DEV) + left.shape[1:])
    right_groups = right.reshape((N_FSDP, TOK_DEV) + right.shape[1:])
    terms = jnp.einsum(form, left_groups, right_groups) * factors.astype(jnp.float32)[None, :, None, None]
    return jnp.sum(rounded(terms), axis=0)


def reference(tokens, cotangent, gate_values, gate_rows, gate_scale, up_values, up_rows, up_scale, down_values, down_cols, down_scale):
    nblocks = D // BLK
    token_total = TOKENS
    x_blocks = tokens.reshape(token_total, nblocks, BLK).astype(jnp.float32)
    grad_blocks = cotangent.reshape(token_total, nblocks, BLK).astype(jnp.float32)
    columns = tuple(jnp.swapaxes(item, 0, 1) for item in (gate_values, gate_rows, gate_scale, up_values, up_rows, up_scale, down_values, down_cols, down_scale))

    def forward(out_sum, column):
        gate_blocks, gate_where, gate_factor, up_blocks, up_where, up_factor, down_blocks, down_where, down_factor = column
        gate_pre = weighted(x_blocks[:, gate_where], gate_blocks, gate_factor)
        up_pre = weighted(x_blocks[:, up_where], up_blocks, up_factor)
        hidden = rounded(gate_pre * jax.nn.sigmoid(gate_pre) * up_pre)
        pieces = jnp.einsum('tb,kbc->tkc', hidden, down_blocks.astype(jnp.float32)) * down_factor.astype(jnp.float32)[None, :, None]
        out_sum = out_sum.at[:, down_where].add(pieces)
        return out_sum, (gate_pre, up_pre, hidden)

    empty_sum = jnp.zeros((token_total, nblocks, BLK), jnp.float32)
    out_sum, saved = lax.scan(forward, empty_sum, columns)
    layer_out = out_sum.reshape(token_total, D).astype(jnp.bfloat16)

    def backward(in_sum, inputs):
        column, kept = inputs
        gate_blocks, gate_where, gate_factor, up_blocks, up_where, up_factor, down_blocks, down_where, down_factor = column
        gate_pre, up_pre, hidden = kept
        down_sel = grad_blocks[:, down_where]
        grad_hidden = jnp.sum(jnp.einsum('tkc,kbc->tkb', down_sel, down_blocks.astype(jnp.float32)) * down_factor.astype(jnp.float32)[None, :, None], axis=1)
        sigmoid_gate = jax.nn.sigmoid(gate_pre)
        grad_gate_act = rounded(grad_hidden * up_pre * sigmoid_gate * (1.0 + gate_pre * (1.0 - sigmoid_gate)))
        grad_up_act = rounded(grad_hidden * gate_pre * sigmoid_gate)
        gate_sel = x_blocks[:, gate_where]
        up_sel = x_blocks[:, up_where]
        down_part = group_sum(hidden, down_sel, 'qtb,qtkc->qkbc', down_factor)
        gate_part = group_sum(gate_sel, grad_gate_act, 'qtka,qtb->qkab', gate_factor)
        up_part = group_sum(up_sel, grad_up_act, 'qtka,qtb->qkab', up_factor)
        back_gate = jnp.einsum('tb,kab->tka', grad_gate_act, gate_blocks.astype(jnp.float32)) * gate_factor.astype(jnp.float32)[None, :, None]
        back_up = jnp.einsum('tb,kab->tka', grad_up_act, up_blocks.astype(jnp.float32)) * up_factor.astype(jnp.float32)[None, :, None]
        in_sum = in_sum.at[:, gate_where].add(back_gate)
        in_sum = in_sum.at[:, up_where].add(back_up)
        return in_sum, (gate_part, up_part, down_part)

    in_sum, grads = lax.scan(backward, empty_sum, (columns, saved))
    grad_tokens = in_sum.reshape(token_total, D).astype(jnp.bfloat16)
    grad_gate = jnp.swapaxes(grads[0], 0, 1).astype(jnp.bfloat16)
    grad_up = jnp.swapaxes(grads[1], 0, 1).astype(jnp.bfloat16)
    grad_down = jnp.swapaxes(grads[2], 0, 1).astype(jnp.bfloat16)
    return (layer_out, grad_tokens, grad_gate, grad_up, grad_down)
```

```python
import functools

import jax
import jax.numpy as jnp
from jax import lax
from jax.experimental import pallas as pl
from jax.experimental.pallas import tpu as pltpu
from jax.sharding import PartitionSpec as P


def scaled_sum(products, factors):
    return jnp.sum(products * factors.astype(jnp.float32)[None, :, :, None], axis=1)


def slot_term(selected, grads, factors):
    return (
        jnp.einsum("tkra,trb->krab", selected, grads, preferred_element_type=jnp.float32)
        * factors[:, :, None, None]
    )


def gathered_plan(
    tokens,
    cotangent,
    gate_values,
    gate_rows,
    gate_scale,
    up_values,
    up_rows,
    up_scale,
    down_values,
    down_cols,
    down_scale,
):
    block_size = gate_values.shape[-1]
    token_count = tokens.shape[0]
    tensor_count = lax.axis_size("tensor")
    nblocks = tokens.shape[1] * tensor_count // block_size
    local_blocks = nblocks // tensor_count
    gathered = lax.all_gather(tokens, "tensor", axis=1, tiled=True)
    x_blocks = gathered.reshape(token_count, nblocks, block_size)
    gate_where, up_where, down_where = (
        lax.all_gather(gate_rows, "fsdp", axis=0, tiled=True),
        lax.all_gather(up_rows, "fsdp", axis=0, tiled=True),
        lax.all_gather(down_cols, "fsdp", axis=0, tiled=True),
    )
    gate_blocks, gate_factor, up_blocks, up_factor, down_blocks, down_factor = (
        lax.all_gather(gate_values, "fsdp", axis=0, tiled=True),
        lax.all_gather(gate_scale, "fsdp", axis=0, tiled=True),
        lax.all_gather(up_values, "fsdp", axis=0, tiled=True),
        lax.all_gather(up_scale, "fsdp", axis=0, tiled=True),
        lax.all_gather(down_values, "fsdp", axis=0, tiled=True),
        lax.all_gather(down_scale, "fsdp", axis=0, tiled=True),
    )
    gate_sel = x_blocks[:, gate_where]
    up_sel = x_blocks[:, up_where]
    gate_pre = scaled_sum(
        jnp.einsum("tkra,krab->tkrb", gate_sel, gate_blocks, preferred_element_type=jnp.float32),
        gate_factor,
    )
    up_pre = scaled_sum(
        jnp.einsum("tkra,krab->tkrb", up_sel, up_blocks, preferred_element_type=jnp.float32),
        up_factor,
    )
    sigmoid_gate = jax.nn.sigmoid(gate_pre)
    activated = gate_pre * sigmoid_gate
    hidden = (activated * up_pre).astype(jnp.bfloat16)
    down_float = down_factor.astype(jnp.float32)
    down_scaled = (
        jnp.einsum("trb,krbc->krtc", hidden, down_blocks, preferred_element_type=jnp.float32)
        * down_float[:, :, None, None]
    )
    out_full = (
        jnp.zeros((nblocks, token_count, block_size), jnp.float32).at[down_where].add(down_scaled)
    )
    out_part = lax.psum_scatter(
        out_full.astype(jnp.bfloat16), "tensor", scatter_dimension=0, tiled=True
    ).astype(jnp.float32)
    layer_out = (
        jnp.transpose(out_part, (1, 0, 2))
        .reshape(token_count, local_blocks * block_size)
        .astype(jnp.bfloat16)
    )
    grad_full = lax.all_gather(cotangent, "tensor", axis=1, tiled=True).reshape(
        token_count, nblocks, block_size
    )
    down_sel = grad_full[:, down_where]
    gate_float = gate_factor.astype(jnp.float32)
    up_float = up_factor.astype(jnp.float32)
    grad_hidden = scaled_sum(
        jnp.einsum("tkrc,krbc->tkrb", down_sel, down_blocks, preferred_element_type=jnp.float32),
        down_factor,
    )
    grad_down = lax.psum_scatter(
        (
            jnp.einsum("trb,tkrc->krbc", hidden, down_sel, preferred_element_type=jnp.float32)
            * down_float[:, :, None, None]
        ).astype(jnp.bfloat16),
        "fsdp",
        scatter_dimension=0,
        tiled=True,
    )
    grad_gate_act = (
        grad_hidden * up_pre * sigmoid_gate * (1.0 + gate_pre * (1.0 - sigmoid_gate))
    ).astype(jnp.bfloat16)
    grad_up_act = (grad_hidden * activated).astype(jnp.bfloat16)
    grad_gate = lax.psum_scatter(
        slot_term(gate_sel, grad_gate_act, gate_float).astype(jnp.bfloat16),
        "fsdp",
        scatter_dimension=0,
        tiled=True,
    )
    grad_up = lax.psum_scatter(
        slot_term(up_sel, grad_up_act, up_float).astype(jnp.bfloat16),
        "fsdp",
        scatter_dimension=0,
        tiled=True,
    )
    back_gate = (
        jnp.einsum("trb,krab->krta", grad_gate_act, gate_blocks, preferred_element_type=jnp.float32)
        * gate_float[:, :, None, None]
    )
    back_up = (
        jnp.einsum("trb,krab->krta", grad_up_act, up_blocks, preferred_element_type=jnp.float32)
        * up_float[:, :, None, None]
    )
    in_full = (
        jnp.zeros((nblocks, token_count, block_size), jnp.float32)
        .at[gate_where]
        .add(back_gate)
        .at[up_where]
        .add(back_up)
    )
    in_part = lax.psum_scatter(
        in_full.astype(jnp.bfloat16), "tensor", scatter_dimension=0, tiled=True
    ).astype(jnp.float32)
    grad_tokens = (
        jnp.transpose(in_part, (1, 0, 2))
        .reshape(token_count, local_blocks * block_size)
        .astype(jnp.bfloat16)
    )
    return (layer_out, grad_tokens, grad_gate, grad_up, grad_down)


def gather_kernel(shards, small, both, wg, wu, wd, tok_all, rg, ru, rd, table, *sems):
    (z_send, z_recv, c_send, c_recv, x_send, x_recv, w_send, w_recv, y_send, y_recv, n_send, n_recv, s_send, s_recv, here) = sems
    part, t, f = lax.axis_index("parts"), lax.axis_index("tensor"), lax.axis_index("fsdp")
    flip = [f, (f // 2) * 2 + 1 - f % 2, (f + 2) % 4, ((f + 2) % 4 // 2) * 2 + 1 - f % 2]
    count = rg.shape[2]
    last = shards - 1
    weights = ((wg, rg), (wu, ru), (wd, rd))

    def to(where, src, dst, send, recv):
        return pltpu.make_async_remote_copy(
            src_ref=src, dst_ref=dst, send_sem=send, recv_sem=recv,
            device_id=where, device_id_type=pl.DeviceIdType.MESH,
        )

    def across(m):
        return (part, t, flip[m])

    over = (1 - part, t, f)
    ups = ((part, t + 1, f), (part, t - 1, f))
    more = (t < last, t > 0)

    barrier = pltpu.get_barrier_semaphore()
    for m in (1, 2, 3):
        pl.semaphore_signal(barrier, inc=1, device_id=across(m), device_id_type=pl.DeviceIdType.MESH)
    pl.semaphore_signal(barrier, inc=1, device_id=over, device_id_type=pl.DeviceIdType.MESH)
    for way in range(2):
        @pl.when(more[way])
        def _():
            pl.semaphore_signal(barrier, inc=1, device_id=ups[way], device_id_type=pl.DeviceIdType.MESH)
    ends = jnp.logical_or(t == 0, t == last)

    @pl.when(ends)
    def _():
        pl.semaphore_wait(barrier, 5)

    @pl.when(jnp.logical_not(ends))
    def _():
        pl.semaphore_wait(barrier, 6)

    def z_copy(way, src, x, own=False):
        source = both if own else tok_all.at[0, src, x]
        return to(ups[way], source, tok_all.at[0, src, x], z_send.at[way, src, x], z_recv.at[way, src, x])

    def c_copy(src, x, own=False):
        source = both if own else tok_all.at[0, src, x]
        return to(across(1), source, tok_all.at[1, src, x], c_send.at[src, x], c_recv.at[src, x])

    x_copy = to(across(2), both, tok_all.at[0, t, 1], x_send, x_recv)
    keep = pltpu.make_async_copy(both, tok_all.at[0, t, 0], here)
    x_copy.start()
    for way in range(2):
        @pl.when(more[way])
        def _():
            z_copy(way, t, 0, True).start()
    tables = [
        to(across(m), small.at[flip[m]], table.at[m - 1], s_send.at[m - 1], s_recv.at[m - 1])
        for m in (1, 2, 3)
    ]
    for c in tables:
        c.start()
    c_copy(t, 0, True).start()
    w_copies, y_copies, y_waits, n_copies = [], [], [], []
    for w, r in weights:
        for m in (2, 3):
            j = len(w_copies)
            w_copies.append(to(across(m), w.at[part, pl.ds(flip[m] * count, count)], r.at[m - 1, part], w_send.at[j], w_recv.at[j]))
            y_copies.append(to(over, r.at[m - 1, part], r.at[m - 1, part], y_send.at[j], y_recv.at[j]))
            y_waits.append(to(over, r.at[m - 1, part], r.at[m - 1, 1 - part], y_send.at[j], y_recv.at[j]))
        for k in range(2):
            j = len(n_copies)
            n_copies.append(to(across(1), w.at[k, pl.ds(flip[1] * count, count)], r.at[0, k], n_send.at[j], n_recv.at[j]))
    for c in w_copies:
        c.start()
    for c in n_copies:
        c.start()
    keep.start()

    x_copy.wait_recv()
    for way in range(2):
        @pl.when(more[way])
        def _():
            z_copy(way, t, 1).start()
    c_copy(t, 1).start()

    def arrive(step, x):
        for way in range(2):
            src = t - step if way == 0 else t + step

            @pl.when(src >= 0 if way == 0 else src <= last)
            def _():
                z_copy(way, src, x).wait_recv()

                @pl.when(more[way])
                def _():
                    z_copy(way, src, x).start()

                c_copy(src, x).start()

    def relay(j):
        w_copies[j].wait_recv()
        y_copies[j].start()

    order = [(s, x) for s in range(1, shards) for x in range(2)]
    done = 0
    for i, (s, x) in enumerate(order):
        arrive(s, x)
        while done < len(w_copies) and done < 2 * i + 1:
            relay(done)
            done += 1
    while done < len(w_copies):
        relay(done)
        done += 1

    for way in range(2):
        for s in range(shards):
            src = t - s if way == 0 else t + s

            @pl.when(jnp.logical_and(src >= 0 if way == 0 else src <= last, more[way]))
            def _():
                for x in range(2):
                    z_copy(way, src, x, s == 0 and x == 0).wait_send()
    for src in range(shards):
        for x in range(2):
            c_copy(src, x).wait_send()
            c_copy(src, x).wait_recv()
    for c in tables + n_copies:
        c.wait_send()
        c.wait_recv()
    x_copy.wait_send()
    for c in w_copies + y_copies:
        c.wait_send()
    for c in y_waits:
        c.wait_recv()
    keep.wait()


def gather(small, both, weights, shards):
    per_dev, local_cols, blk, _ = weights[0].shape
    count = local_cols // 4
    bf = jnp.bfloat16
    dma = lambda *a: pltpu.SemaphoreType.DMA(a)
    received = jax.ShapeDtypeStruct((3, per_dev, count, blk, blk), bf)
    anywhere = pl.BlockSpec(memory_space=pl.ANY)
    z = (2, shards, 2)
    c = (shards, 2)
    one = pltpu.SemaphoreType.DMA
    return pl.pallas_call(
        functools.partial(gather_kernel, shards),
        out_shape=[
            jax.ShapeDtypeStruct((2, shards, 2) + both.shape, bf),
            received, received, received,
            jax.ShapeDtypeStruct((3,) + small.shape[1:], jnp.float32),
        ],
        in_specs=[anywhere] * 5,
        out_specs=[anywhere] * 5,
        scratch_shapes=[dma(*z), dma(*z), dma(*c), dma(*c), one, one, dma(6), dma(6), dma(6), dma(6), dma(6), dma(6), dma(3), dma(3), one],
        compiler_params=pltpu.CompilerParams(collective_id=0, has_side_effects=True),
    )(small, both, *weights)


NN = (((1,), (0,)), ((), ()))
NT = (((1,), (1,)), ((), ()))
dot = functools.partial(lax.dot_general, preferred_element_type=jnp.float32)


def load(rows_ref, tok_ref, tok, which, array, slot, sel):
    per_shard, blk = tok_ref.shape[4], tok_ref.shape[6]
    place = rows_ref[array, slot, pl.program_id(0)]
    shard, block = place // per_shard, place % per_shard
    for c in range(2):
        for x in range(2):
            q = c * 2 + x
            sel[q * tok : (q + 1) * tok, slot * blk : (slot + 1) * blk] = tok_ref[c, shard, x, which, block]


def scaled(scale_ref, own, recv, array, slot):
    per_dev = own.shape[0]
    src, sub = slot // per_dev, slot % per_dev
    value = recv[src - 1, sub, 0] if src else own[sub, 0]
    return (value.astype(jnp.float32) * scale_ref[array, slot, pl.program_id(0)]).astype(jnp.bfloat16)


def accumulate(rows_ref, acc, array, slots, blk, product):
    for slot in range(slots):
        acc[rows_ref[array, slot, pl.program_id(0)]] += product[:, slot * blk : (slot + 1) * blk]


def clear(acc):
    @pl.when(pl.program_id(0) == 0)
    def _():
        acc[...] = jnp.zeros_like(acc)


def flush(place_ref, acc, tok, own, other):
    per_shard = own[0].shape[1]

    @pl.when(pl.program_id(0) == pl.num_programs(0) - 1)
    def _():
        for m in range(len(own)):
            first = (place_ref[1] ^ m) * per_shard
            for c, ref in enumerate((own[m], other[m])):
                for x in range(2):
                    q = c * 2 + x

                    @pl.loop(0, per_shard)
                    def _(d):
                        ref[x, d] = acc[first + d, q * tok : (q + 1) * tok, :].astype(jnp.bfloat16)


def early_kernel(dims, rows_ref, scale_ref, place_ref, tok_ref, *refs):
    slots, per_dev, tok, blk, shards = dims
    nsrc = slots // per_dev
    own_w, recv_w, refs = refs[:3], refs[3:6], refs[6:]
    grads, (gate_pre_ref, up_pre_ref), refs = refs[:nsrc], refs[nsrc : nsrc + 2], refs[nsrc + 2 :]
    own, other, scratch = refs[:shards], refs[shards : 2 * shards], refs[2 * shards :]
    acc, gate_sel, up_sel, down_sel, gate_w, up_w, down_w = scratch
    r = pl.program_id(0)
    clear(acc)
    for slot in range(slots):
        span = slice(slot * blk, (slot + 1) * blk)
        load(rows_ref, tok_ref, tok, 0, 0, slot, gate_sel)
        load(rows_ref, tok_ref, tok, 0, 1, slot, up_sel)
        load(rows_ref, tok_ref, tok, 1, 2, slot, down_sel)
        gate_w[span, :] = scaled(scale_ref, own_w[0], recv_w[0], 0, slot)
        up_w[span, :] = scaled(scale_ref, own_w[1], recv_w[1], 1, slot)
        down_w[:, span] = scaled(scale_ref, own_w[2], recv_w[2], 2, slot)
    gate_pre = dot(gate_sel[...], gate_w[...], NN)
    up_pre = dot(up_sel[...], up_w[...], NN)
    gate_pre_ref[0], up_pre_ref[0] = gate_pre, up_pre
    hidden = (gate_pre * jax.nn.sigmoid(gate_pre) * up_pre).astype(jnp.bfloat16)
    down = dot(hidden.T, down_sel[...], NN)
    for slot in range(slots):
        src, sub = slot // per_dev, slot % per_dev
        g = down[:, slot * blk : (slot + 1) * blk] * scale_ref[2, slot, r]
        grads[src][sub, 0] = g.astype(jnp.bfloat16)
    accumulate(rows_ref, acc, 2, slots, blk, dot(hidden, down_w[...], NN))
    flush(place_ref, acc, tok, own, other)


def middle_kernel(dims, rows_ref, scale_ref, place_ref, tok_ref, own_w, recv_w, gate_pre_ref, up_pre_ref, *refs):
    slots, per_dev, tok, blk, _ = dims
    nsrc = slots // per_dev
    grads, (gate_act_ref, up_act_ref), scratch = (refs[:nsrc], refs[nsrc : 2 * nsrc]), refs[2 * nsrc : 2 * nsrc + 2], refs[2 * nsrc + 2 :]
    gate_sel, up_sel, down_sel, down_w = scratch
    r = pl.program_id(0)
    for slot in range(slots):
        load(rows_ref, tok_ref, tok, 0, 0, slot, gate_sel)
        load(rows_ref, tok_ref, tok, 0, 1, slot, up_sel)
        load(rows_ref, tok_ref, tok, 1, 2, slot, down_sel)
        down_w[:, slot * blk : (slot + 1) * blk] = scaled(scale_ref, own_w, recv_w, 2, slot)
    gate_pre, up_pre = gate_pre_ref[0], up_pre_ref[0]
    grad_hidden = dot(down_sel[...], down_w[...], NT)
    sig = jax.nn.sigmoid(gate_pre)
    act = gate_pre * sig
    gate_act = (grad_hidden * up_pre * sig * (1.0 + gate_pre * (1.0 - sig))).astype(jnp.bfloat16)
    up_act = (grad_hidden * act).astype(jnp.bfloat16)
    gate_act_ref[0], up_act_ref[0] = gate_act, up_act
    for slot in range(slots):
        span = slice(slot * blk, (slot + 1) * blk)
        src, sub = slot // per_dev, slot % per_dev
        g = dot(gate_sel[:, span].T, gate_act, NN) * scale_ref[0, slot, r]
        grads[0][src][sub, 0] = g.astype(jnp.bfloat16)
        g = dot(up_sel[:, span].T, up_act, NN) * scale_ref[1, slot, r]
        grads[1][src][sub, 0] = g.astype(jnp.bfloat16)


def late_kernel(dims, rows_ref, scale_ref, place_ref, *refs):
    slots, _, tok, blk, shards = dims
    own_w, recv_w, (gate_act_ref, up_act_ref), refs = refs[:2], refs[2:4], refs[4:6], refs[6:]
    own, other, (acc, gate_w, up_w) = refs[:shards], refs[shards : 2 * shards], refs[2 * shards :]
    clear(acc)
    for slot in range(slots):
        span = slice(slot * blk, (slot + 1) * blk)
        gate_w[span, :] = scaled(scale_ref, own_w[0], recv_w[0], 0, slot)
        up_w[span, :] = scaled(scale_ref, own_w[1], recv_w[1], 1, slot)
    accumulate(rows_ref, acc, 0, slots, blk, dot(gate_act_ref[0], gate_w[...], NT))
    accumulate(rows_ref, acc, 1, slots, blk, dot(up_act_ref[0], up_w[...], NT))
    flush(place_ref, acc, tok, own, other)


def columns(which, scalars, tok_all, own_w, recv_w, kept):
    nsrc = 1 + recv_w[0].shape[0]
    _, per_dev, count, blk, _ = recv_w[0].shape
    _, shards, _, _, per_shard, tok, _ = tok_all.shape
    nblk = shards * per_shard
    slots = per_dev * nsrc
    total = 4 * tok
    bf, f32 = jnp.bfloat16, jnp.float32
    whole = lambda a: pl.BlockSpec(a, lambda r, *_: (0,) * len(a), pipeline_mode=pl.Buffered(1))
    own_block = pl.BlockSpec((per_dev, 1, blk, blk), lambda r, rows, scale, at: (0, at[0] * count + r, 0, 0))
    recv_block = pl.BlockSpec((nsrc - 1, per_dev, 1, blk, blk), lambda r, *_: (0, 0, r, 0, 0))
    block = pl.BlockSpec((per_dev, 1, blk, blk), lambda r, *_: (0, r, 0, 0))
    piece = jax.ShapeDtypeStruct((per_dev, count, blk, blk), bf)
    kept_block = [pl.BlockSpec((1, total, blk), lambda r, *_: (r, 0, 0))] * 2
    keep = lambda kind: [jax.ShapeDtypeStruct((count, total, blk), kind)] * 2
    sum_block = [whole((2, per_shard, tok, blk))] * (2 * shards)
    sums = [jax.ShapeDtypeStruct((2, per_shard, tok, blk), bf)] * (2 * shards)
    acc = pltpu.VMEM((nblk, total, blk), f32)
    sel = pltpu.VMEM((total, slots * blk), bf)
    tall, wide = pltpu.VMEM((slots * blk, blk), bf), pltpu.VMEM((blk, slots * blk), bf)
    if which == "early":
        body, products = early_kernel, 4
        in_specs = [whole(tok_all.shape)] + [own_block] * 3 + [recv_block] * 3
        operands = (tok_all, *own_w, *recv_w)
        out_specs, out_shape = [block] * nsrc + kept_block + sum_block, [piece] * nsrc + keep(f32) + sums
        scratch = [acc, sel, sel, sel, tall, tall, wide]
    elif which == "middle":
        body, products = middle_kernel, 3
        in_specs = [whole(tok_all.shape), own_block, recv_block] + kept_block
        operands = (tok_all, own_w[2], recv_w[2], *kept)
        out_specs, out_shape = [block] * (2 * nsrc) + kept_block, [piece] * (2 * nsrc) + keep(bf)
        scratch = [sel, sel, sel, wide]
    else:
        body, products = late_kernel, 2
        in_specs = [own_block] * 2 + [recv_block] * 2 + kept_block
        operands = (*own_w[:2], *recv_w[:2], *kept)
        out_specs, out_shape = sum_block, sums
        scratch = [acc, tall, tall]
    flops = 2 * products * slots * count * total * blk * blk
    return pl.pallas_call(
        functools.partial(body, (slots, per_dev, tok, blk, shards)),
        grid_spec=pltpu.PrefetchScalarGridSpec(
            num_scalar_prefetch=3, grid=(count,), in_specs=in_specs, out_specs=out_specs, scratch_shapes=scratch,
        ),
        out_shape=out_shape,
        compiler_params=pltpu.CompilerParams(vmem_limit_bytes=60 * 1024 * 1024),
        cost_estimate=pl.CostEstimate(flops=flops, bytes_accessed=40 << 20, transcendentals=0),
    )(*scalars, *operands)


def swap(value, flip, axis="fsdp"):
    return lax.ppermute(value, axis, [(i, i ^ flip) for i in range(lax.axis_size(axis))])


def exchanged_plan(
    tokens,
    cotangent,
    gate_values,
    gate_rows,
    gate_scale,
    up_values,
    up_rows,
    up_scale,
    down_values,
    down_cols,
    down_scale,
):
    tok, width = tokens.shape
    per_dev, local_cols, blk, _ = gate_values.shape
    count = local_cols // 4
    mine, shard = lax.axis_index("fsdp"), lax.axis_index("tensor")
    f32, bf = jnp.float32, jnp.bfloat16

    shards = lax.axis_size("tensor")
    both = jnp.stack([tokens, cotangent]).reshape(2, tok, width // blk, blk).transpose(0, 2, 1, 3)
    small = jnp.stack(
        [a.astype(f32) for a in (gate_rows, up_rows, down_cols, gate_scale, up_scale, down_scale)]
    )
    small = small.reshape(6, per_dev, 4, count).transpose(2, 0, 1, 3)
    own_w = (gate_values, up_values, down_values)
    tok_all, *recv_w, table = gather(small, both, own_w, shards)
    kept = lax.dynamic_slice_in_dim(small, mine, 1, axis=0)
    table = jnp.concatenate([kept, table]).transpose(1, 0, 2, 3).reshape(6, 4 * per_dev, count)
    table_rows = table[:3].astype(jnp.int32)
    table_scale = table[3:]

    def home(pieces):
        result = jnp.zeros((per_dev, local_cols, blk, blk), bf)
        for m, part in enumerate(pieces):
            result = lax.dynamic_update_slice_in_dim(result, part, (mine ^ m) * count, axis=1)
        return result

    def send(pieces):
        return [p if m == 0 else swap(p, m) for m, p in enumerate(pieces)]

    def chip_sum(own, other):
        return [(a.astype(f32) + swap(b, 1).astype(f32)).astype(bf) for a, b in zip(own, other)]

    def scatter(chip):
        return [c if m == 0 else swap(c, m, "tensor") for m, c in enumerate(chip)]

    def finish(shares):
        far = sum(s[1].astype(f32) for s in shares).astype(bf)
        total = (sum(s[0].astype(f32) for s in shares) + swap(far, 2).astype(f32)).astype(bf)
        return total.transpose(1, 0, 2).reshape(tok, width)

    scalars = (table_rows, table_scale, jnp.stack([mine, shard]).astype(jnp.int32))
    early = columns("early", scalars, tok_all, own_w, recv_w, ())
    down_pieces, pre, own, other = early[:4], early[4:6], early[6 : 6 + shards], early[6 + shards :]
    chip = chip_sum(own, other)
    down_sent = send(down_pieces)
    chip, pre = lax.optimization_barrier((chip, pre))
    out_shares = scatter(chip)
    middle = columns("middle", scalars, tok_all, own_w, recv_w, pre)
    gate_sent, up_sent = send(middle[:4]), send(middle[4:8])
    late = columns("late", scalars, tok_all, own_w, recv_w, middle[8:])
    chip = chip_sum(late[:shards], late[shards:])
    in_shares = scatter(chip)
    return (finish(out_shares), finish(in_shares), home(gate_sent), home(up_sent), home(down_sent))


def choose_plan(mesh, *args):
    fits = mesh.shape["fsdp"] == 4 and mesh.shape["parts"] == 2 and args[2].shape[0] == 2
    fits = fits and args[2].shape[1] % 4 == 0 and mesh.shape["tensor"] in (2, 4, 8)
    plan = exchanged_plan if fits else gathered_plan
    return plan(*args)


def solution(mesh):
    plan = functools.partial(choose_plan, mesh)
    in_specs = (
        P(("parts", "fsdp"), "tensor"),
        P(("parts", "fsdp"), "tensor"),
        P("fsdp", "tensor", None, None),
        P("fsdp", "tensor"),
        P("fsdp", "tensor"),
        P("fsdp", "tensor", None, None),
        P("fsdp", "tensor"),
        P("fsdp", "tensor"),
        P("fsdp", "tensor", None, None),
        P("fsdp", "tensor"),
        P("fsdp", "tensor"),
    )
    out_specs = (
        P(("parts", "fsdp"), "tensor"),
        P(("parts", "fsdp"), "tensor"),
        P(("parts", "fsdp"), "tensor", None, None),
        P(("parts", "fsdp"), "tensor", None, None),
        P(("parts", "fsdp"), "tensor", None, None),
    )
    return jax.shard_map(plan, mesh=mesh, in_specs=in_specs, out_specs=out_specs, check_vma=False)
```

```python
import functools

import jax
import jax.numpy as jnp
from jax import lax
from jax.experimental import pallas as pl
from jax.experimental.pallas import tpu as pltpu
from jax.sharding import PartitionSpec as P


def scaled_sum(products, factors):
    return jnp.sum(products * factors.astype(jnp.float32)[None, :, :, None], axis=1)


def slot_term(selected, grads, factors):
    return (
        jnp.einsum("tkra,trb->krab", selected, grads, preferred_element_type=jnp.float32)
        * factors[:, :, None, None]
    )


def gathered_plan(
    tokens,
    cotangent,
    gate_values,
    gate_rows,
    gate_scale,
    up_values,
    up_rows,
    up_scale,
    down_values,
    down_cols,
    down_scale,
):
    block_size = gate_values.shape[-1]
    token_count = tokens.shape[0]
    tensor_count = lax.axis_size("tensor")
    nblocks = tokens.shape[1] * tensor_count // block_size
    local_blocks = nblocks // tensor_count
    gathered = lax.all_gather(tokens, "tensor", axis=1, tiled=True)
    x_blocks = gathered.reshape(token_count, nblocks, block_size)
    gate_where, up_where, down_where = (
        lax.all_gather(gate_rows, "fsdp", axis=0, tiled=True),
        lax.all_gather(up_rows, "fsdp", axis=0, tiled=True),
        lax.all_gather(down_cols, "fsdp", axis=0, tiled=True),
    )
    gate_blocks, gate_factor, up_blocks, up_factor, down_blocks, down_factor = (
        lax.all_gather(gate_values, "fsdp", axis=0, tiled=True),
        lax.all_gather(gate_scale, "fsdp", axis=0, tiled=True),
        lax.all_gather(up_values, "fsdp", axis=0, tiled=True),
        lax.all_gather(up_scale, "fsdp", axis=0, tiled=True),
        lax.all_gather(down_values, "fsdp", axis=0, tiled=True),
        lax.all_gather(down_scale, "fsdp", axis=0, tiled=True),
    )
    gate_sel = x_blocks[:, gate_where]
    up_sel = x_blocks[:, up_where]
    gate_pre = scaled_sum(
        jnp.einsum("tkra,krab->tkrb", gate_sel, gate_blocks, preferred_element_type=jnp.float32),
        gate_factor,
    )
    up_pre = scaled_sum(
        jnp.einsum("tkra,krab->tkrb", up_sel, up_blocks, preferred_element_type=jnp.float32),
        up_factor,
    )
    sigmoid_gate = jax.nn.sigmoid(gate_pre)
    activated = gate_pre * sigmoid_gate
    hidden = (activated * up_pre).astype(jnp.bfloat16)
    down_float = down_factor.astype(jnp.float32)
    down_scaled = (
        jnp.einsum("trb,krbc->krtc", hidden, down_blocks, preferred_element_type=jnp.float32)
        * down_float[:, :, None, None]
    )
    out_full = (
        jnp.zeros((nblocks, token_count, block_size), jnp.float32).at[down_where].add(down_scaled)
    )
    out_part = lax.psum_scatter(
        out_full.astype(jnp.bfloat16), "tensor", scatter_dimension=0, tiled=True
    ).astype(jnp.float32)
    layer_out = (
        jnp.transpose(out_part, (1, 0, 2))
        .reshape(token_count, local_blocks * block_size)
        .astype(jnp.bfloat16)
    )
    grad_full = lax.all_gather(cotangent, "tensor", axis=1, tiled=True).reshape(
        token_count, nblocks, block_size
    )
    down_sel = grad_full[:, down_where]
    gate_float = gate_factor.astype(jnp.float32)
    up_float = up_factor.astype(jnp.float32)
    grad_hidden = scaled_sum(
        jnp.einsum("tkrc,krbc->tkrb", down_sel, down_blocks, preferred_element_type=jnp.float32),
        down_factor,
    )
    grad_down = lax.psum_scatter(
        (
            jnp.einsum("trb,tkrc->krbc", hidden, down_sel, preferred_element_type=jnp.float32)
            * down_float[:, :, None, None]
        ).astype(jnp.bfloat16),
        "fsdp",
        scatter_dimension=0,
        tiled=True,
    )
    grad_gate_act = (
        grad_hidden * up_pre * sigmoid_gate * (1.0 + gate_pre * (1.0 - sigmoid_gate))
    ).astype(jnp.bfloat16)
    grad_up_act = (grad_hidden * activated).astype(jnp.bfloat16)
    grad_gate = lax.psum_scatter(
        slot_term(gate_sel, grad_gate_act, gate_float).astype(jnp.bfloat16),
        "fsdp",
        scatter_dimension=0,
        tiled=True,
    )
    grad_up = lax.psum_scatter(
        slot_term(up_sel, grad_up_act, up_float).astype(jnp.bfloat16),
        "fsdp",
        scatter_dimension=0,
        tiled=True,
    )
    back_gate = (
        jnp.einsum("trb,krab->krta", grad_gate_act, gate_blocks, preferred_element_type=jnp.float32)
        * gate_float[:, :, None, None]
    )
    back_up = (
        jnp.einsum("trb,krab->krta", grad_up_act, up_blocks, preferred_element_type=jnp.float32)
        * up_float[:, :, None, None]
    )
    in_full = (
        jnp.zeros((nblocks, token_count, block_size), jnp.float32)
        .at[gate_where]
        .add(back_gate)
        .at[up_where]
        .add(back_up)
    )
    in_part = lax.psum_scatter(
        in_full.astype(jnp.bfloat16), "tensor", scatter_dimension=0, tiled=True
    ).astype(jnp.float32)
    grad_tokens = (
        jnp.transpose(in_part, (1, 0, 2))
        .reshape(token_count, local_blocks * block_size)
        .astype(jnp.bfloat16)
    )
    return (layer_out, grad_tokens, grad_gate, grad_up, grad_down)


def gather_kernel(shards, small, both, wg, wu, wd, tok_all, rg, ru, rd, table, *sems):
    (z_send, z_recv, c_send, c_recv, x_send, x_recv, w_send, w_recv, y_send, y_recv, n_send, n_recv, s_send, s_recv, here) = sems
    part, t, f = lax.axis_index("parts"), lax.axis_index("tensor"), lax.axis_index("fsdp")
    flip = [f, (f // 2) * 2 + 1 - f % 2, (f + 2) % 4, ((f + 2) % 4 // 2) * 2 + 1 - f % 2]
    count = rg.shape[2]
    last = shards - 1
    weights = ((wg, rg), (wu, ru), (wd, rd))

    def to(where, src, dst, send, recv):
        return pltpu.make_async_remote_copy(
            src_ref=src, dst_ref=dst, send_sem=send, recv_sem=recv,
            device_id=where, device_id_type=pl.DeviceIdType.MESH,
        )

    def across(m):
        return (part, t, flip[m])

    over = (1 - part, t, f)
    ups = ((part, t + 1, f), (part, t - 1, f))
    more = (t < last, t > 0)

    barrier = pltpu.get_barrier_semaphore()
    for m in (1, 2, 3):
        pl.semaphore_signal(barrier, inc=1, device_id=across(m), device_id_type=pl.DeviceIdType.MESH)
    pl.semaphore_signal(barrier, inc=1, device_id=over, device_id_type=pl.DeviceIdType.MESH)
    for way in range(2):
        @pl.when(more[way])
        def _():
            pl.semaphore_signal(barrier, inc=1, device_id=ups[way], device_id_type=pl.DeviceIdType.MESH)
    ends = jnp.logical_or(t == 0, t == last)

    @pl.when(ends)
    def _():
        pl.semaphore_wait(barrier, 5)

    @pl.when(jnp.logical_not(ends))
    def _():
        pl.semaphore_wait(barrier, 6)

    def z_copy(way, src, x, own=False):
        source = both if own else tok_all.at[0, src, x]
        return to(ups[way], source, tok_all.at[0, src, x], z_send.at[way, src, x], z_recv.at[way, src, x])

    def c_copy(src, x, own=False):
        source = both if own else tok_all.at[0, src, x]
        return to(across(1), source, tok_all.at[1, src, x], c_send.at[src, x], c_recv.at[src, x])

    x_copy = to(across(2), both, tok_all.at[0, t, 1], x_send, x_recv)
    keep = pltpu.make_async_copy(both, tok_all.at[0, t, 0], here)
    x_copy.start()
    for way in range(2):
        @pl.when(more[way])
        def _():
            z_copy(way, t, 0, True).start()
    tables = [
        to(across(m), small.at[flip[m]], table.at[m - 1], s_send.at[m - 1], s_recv.at[m - 1])
        for m in (1, 2, 3)
    ]
    for c in tables:
        c.start()
    c_copy(t, 0, True).start()
    w_copies, y_copies, y_waits, n_copies = [], [], [], []
    for w, r in weights:
        for m in (2, 3):
            j = len(w_copies)
            w_copies.append(to(across(m), w.at[part, pl.ds(flip[m] * count, count)], r.at[m - 1, part], w_send.at[j], w_recv.at[j]))
            y_copies.append(to(over, r.at[m - 1, part], r.at[m - 1, part], y_send.at[j], y_recv.at[j]))
            y_waits.append(to(over, r.at[m - 1, part], r.at[m - 1, 1 - part], y_send.at[j], y_recv.at[j]))
        for k in range(2):
            j = len(n_copies)
            n_copies.append(to(across(1), w.at[k, pl.ds(flip[1] * count, count)], r.at[0, k], n_send.at[j], n_recv.at[j]))
    for c in w_copies:
        c.start()
    for c in n_copies:
        c.start()
    keep.start()

    x_copy.wait_recv()
    for way in range(2):
        @pl.when(more[way])
        def _():
            z_copy(way, t, 1).start()
    c_copy(t, 1).start()

    def arrive(step, x):
        for way in range(2):
            src = t - step if way == 0 else t + step

            @pl.when(src >= 0 if way == 0 else src <= last)
            def _():
                z_copy(way, src, x).wait_recv()

                @pl.when(more[way])
                def _():
                    z_copy(way, src, x).start()

                c_copy(src, x).start()

    def relay(j):
        w_copies[j].wait_recv()
        y_copies[j].start()

    order = [(s, x) for s in range(1, shards) for x in range(2)]
    done = 0
    for i, (s, x) in enumerate(order):
        arrive(s, x)
        while done < len(w_copies) and done < 2 * i + 1:
            relay(done)
            done += 1
    while done < len(w_copies):
        relay(done)
        done += 1

    for way in range(2):
        for s in range(shards):
            src = t - s if way == 0 else t + s

            @pl.when(jnp.logical_and(src >= 0 if way == 0 else src <= last, more[way]))
            def _():
                for x in range(2):
                    z_copy(way, src, x, s == 0 and x == 0).wait_send()
    for src in range(shards):
        for x in range(2):
            c_copy(src, x).wait_send()
            c_copy(src, x).wait_recv()
    for c in tables + n_copies:
        c.wait_send()
        c.wait_recv()
    x_copy.wait_send()
    for c in w_copies + y_copies:
        c.wait_send()
    for c in y_waits:
        c.wait_recv()
    keep.wait()


def gather(small, both, weights, shards):
    per_dev, local_cols, blk, _ = weights[0].shape
    count = local_cols // 4
    bf = jnp.bfloat16
    dma = lambda *a: pltpu.SemaphoreType.DMA(a)
    received = jax.ShapeDtypeStruct((3, per_dev, count, blk, blk), bf)
    anywhere = pl.BlockSpec(memory_space=pl.ANY)
    z = (2, shards, 2)
    c = (shards, 2)
    one = pltpu.SemaphoreType.DMA
    return pl.pallas_call(
        functools.partial(gather_kernel, shards),
        out_shape=[
            jax.ShapeDtypeStruct((2, shards, 2) + both.shape, bf),
            received, received, received,
            jax.ShapeDtypeStruct((3,) + small.shape[1:], jnp.float32),
        ],
        in_specs=[anywhere] * 5,
        out_specs=[anywhere] * 5,
        scratch_shapes=[dma(*z), dma(*z), dma(*c), dma(*c), one, one, dma(6), dma(6), dma(6), dma(6), dma(6), dma(6), dma(3), dma(3), one],
        compiler_params=pltpu.CompilerParams(collective_id=0, has_side_effects=True),
    )(small, both, *weights)


NN = (((1,), (0,)), ((), ()))
NT = (((1,), (1,)), ((), ()))
dot = functools.partial(lax.dot_general, preferred_element_type=jnp.float32)


def load(rows_ref, tok_ref, tok, which, array, slot, r, sel):
    per_shard, blk = tok_ref.shape[4], tok_ref.shape[6]
    place = rows_ref[array, slot, r]
    shard, block = place // per_shard, place % per_shard
    for c in range(2):
        for x in range(2):
            q = c * 2 + x
            sel[q * tok : (q + 1) * tok, slot * blk : (slot + 1) * blk] = tok_ref[c, shard, x, which, block]


def scaled(scale_ref, own, recv, array, slot, r):
    per_dev = own.shape[0]
    src, sub = slot // per_dev, slot % per_dev
    value = recv[src - 1, sub, 0] if src else own[sub, 0]
    return (value.astype(jnp.float32) * scale_ref[array, slot, r]).astype(jnp.bfloat16)


def accumulate(rows_ref, acc, array, slots, blk, product):
    for slot in range(slots):
        acc[rows_ref[array, slot, pl.program_id(0)]] += product[:, slot * blk : (slot + 1) * blk]


def clear(acc):
    @pl.when(pl.program_id(0) == 0)
    def _():
        acc[...] = jnp.zeros_like(acc)


def flush(shard, acc, tok, own, other):
    per_shard = own[0].shape[1]

    @pl.when(pl.program_id(0) == pl.num_programs(0) - 1)
    def _():
        for m in range(len(own)):
            first = (shard ^ m) * per_shard
            for c, ref in enumerate((own[m], other[m])):
                for x in range(2):
                    q = c * 2 + x

                    @pl.loop(0, per_shard)
                    def _(d):
                        ref[x, d] = acc[first + d, q * tok : (q + 1) * tok, :].astype(jnp.bfloat16)


def early_kernel(dims, rows_ref, scale_ref, place_ref, tok_ref, *refs):
    slots, per_dev, tok, blk, shards = dims
    nsrc = slots // per_dev
    own_w, recv_w, refs = refs[:3], refs[3:6], refs[6:]
    grads, (gate_pre_ref, up_pre_ref), refs = refs[:nsrc], refs[nsrc : nsrc + 2], refs[nsrc + 2 :]
    own, other, scratch = refs[:shards], refs[shards : 2 * shards], refs[2 * shards :]
    acc, gate_sel, up_sel, down_sel, gate_w, up_w, down_w = scratch
    r = pl.program_id(0)
    clear(acc)
    for slot in range(slots):
        span = slice(slot * blk, (slot + 1) * blk)
        load(rows_ref, tok_ref, tok, 0, 0, slot, r, gate_sel)
        load(rows_ref, tok_ref, tok, 0, 1, slot, r, up_sel)
        load(rows_ref, tok_ref, tok, 1, 2, slot, r, down_sel)
        gate_w[span, :] = scaled(scale_ref, own_w[0], recv_w[0], 0, slot, r)
        up_w[span, :] = scaled(scale_ref, own_w[1], recv_w[1], 1, slot, r)
        down_w[:, span] = scaled(scale_ref, own_w[2], recv_w[2], 2, slot, r)
    gate_pre = dot(gate_sel[...], gate_w[...], NN)
    up_pre = dot(up_sel[...], up_w[...], NN)
    gate_pre_ref[0], up_pre_ref[0] = gate_pre, up_pre
    hidden = (gate_pre * jax.nn.sigmoid(gate_pre) * up_pre).astype(jnp.bfloat16)
    down = dot(hidden.T, down_sel[...], NN)
    for slot in range(slots):
        src, sub = slot // per_dev, slot % per_dev
        g = down[:, slot * blk : (slot + 1) * blk] * scale_ref[2, slot, r]
        grads[src][sub, 0] = g.astype(jnp.bfloat16)
    accumulate(rows_ref, acc, 2, slots, blk, dot(hidden, down_w[...], NN))
    flush(place_ref[1], acc, tok, own, other)


def middle_kernel(dims, begin, rows_ref, scale_ref, place_ref, tok_ref, own_w, recv_w, gate_pre_ref, up_pre_ref, *refs):
    slots, per_dev, tok, blk, _ = dims
    nsrc = slots // per_dev
    grads, (gate_act_ref, up_act_ref), scratch = (refs[:nsrc], refs[nsrc : 2 * nsrc]), refs[2 * nsrc : 2 * nsrc + 2], refs[2 * nsrc + 2 :]
    gate_sel, up_sel, down_sel, down_w = scratch
    r = pl.program_id(0) + begin
    for slot in range(slots):
        load(rows_ref, tok_ref, tok, 0, 0, slot, r, gate_sel)
        load(rows_ref, tok_ref, tok, 0, 1, slot, r, up_sel)
        load(rows_ref, tok_ref, tok, 1, 2, slot, r, down_sel)
        down_w[:, slot * blk : (slot + 1) * blk] = scaled(scale_ref, own_w, recv_w, 2, slot, r)
    gate_pre, up_pre = gate_pre_ref[0], up_pre_ref[0]
    grad_hidden = dot(down_sel[...], down_w[...], NT)
    sig = jax.nn.sigmoid(gate_pre)
    act = gate_pre * sig
    gate_act = (grad_hidden * up_pre * sig * (1.0 + gate_pre * (1.0 - sig))).astype(jnp.bfloat16)
    up_act = (grad_hidden * act).astype(jnp.bfloat16)
    gate_act_ref[0], up_act_ref[0] = gate_act, up_act
    for slot in range(slots):
        span = slice(slot * blk, (slot + 1) * blk)
        src, sub = slot // per_dev, slot % per_dev
        g = dot(gate_sel[:, span].T, gate_act, NN) * scale_ref[0, slot, r]
        grads[0][src][sub, 0] = g.astype(jnp.bfloat16)
        g = dot(up_sel[:, span].T, up_act, NN) * scale_ref[1, slot, r]
        grads[1][src][sub, 0] = g.astype(jnp.bfloat16)


def late_kernel(dims, splits, rows_ref, scale_ref, place_ref, *refs):
    slots, _, tok, blk, shards = dims
    own_w, recv_w, refs = refs[:2], refs[2:4], refs[4:]
    kept, refs = refs[: 2 * len(splits)], refs[2 * len(splits) :]
    own_ref, other_ref, acc, gate_w, up_w = refs
    own, other = [own_ref.at[d] for d in range(shards)], [other_ref.at[d] for d in range(shards)]
    r = pl.program_id(0)
    clear(acc)
    for slot in range(slots):
        span = slice(slot * blk, (slot + 1) * blk)
        gate_w[span, :] = scaled(scale_ref, own_w[0], recv_w[0], 0, slot, r)
        up_w[span, :] = scaled(scale_ref, own_w[1], recv_w[1], 1, slot, r)
    for i, begin in enumerate(splits):
        end = splits[i + 1] if i + 1 < len(splits) else pl.num_programs(0)

        @pl.when(jnp.logical_and(r >= begin, r < end))
        def _():
            accumulate(rows_ref, acc, 0, slots, blk, dot(kept[2 * i][0], gate_w[...], NT))
            accumulate(rows_ref, acc, 1, slots, blk, dot(kept[2 * i + 1][0], up_w[...], NT))

    flush(0, acc, tok, own, other)


def columns(which, scalars, tok_all, own_w, recv_w, kept, splits):
    nsrc = 1 + recv_w[0].shape[0]
    _, per_dev, count, blk, _ = recv_w[0].shape
    _, shards, _, _, per_shard, tok, _ = tok_all.shape
    nblk = shards * per_shard
    slots = per_dev * nsrc
    total = 4 * tok
    bf, f32 = jnp.bfloat16, jnp.float32
    ends = splits[1:] + (count,)
    begin, steps = (splits[which], ends[which] - splits[which]) if isinstance(which, int) else (0, count)
    whole = lambda a: pl.BlockSpec(a, lambda r, *_: (0,) * len(a), pipeline_mode=pl.Buffered(1))
    own_block = pl.BlockSpec((per_dev, 1, blk, blk), lambda r, rows, scale, at: (0, at[0] * count + begin + r, 0, 0))
    recv_block = pl.BlockSpec((nsrc - 1, per_dev, 1, blk, blk), lambda r, *_: (0, 0, begin + r, 0, 0))
    block = pl.BlockSpec((per_dev, 1, blk, blk), lambda r, *_: (0, r, 0, 0))
    piece = jax.ShapeDtypeStruct((per_dev, steps, blk, blk), bf)
    clipped = lambda low, size: pl.BlockSpec((1, total, blk), lambda r, *_: (jnp.clip(r - low, 0, size - 1), 0, 0))
    keep = lambda kind: [jax.ShapeDtypeStruct((steps, total, blk), kind)] * 2
    share = (2, per_shard, tok, blk)
    acc = pltpu.VMEM((nblk, total, blk), f32)
    sel = pltpu.VMEM((total, slots * blk), bf)
    tall, wide = pltpu.VMEM((slots * blk, blk), bf), pltpu.VMEM((blk, slots * blk), bf)
    dims = (slots, per_dev, tok, blk, shards)
    if which == "early":
        body, products = functools.partial(early_kernel, dims), 4
        in_specs = [whole(tok_all.shape)] + [own_block] * 3 + [recv_block] * 3
        operands = (tok_all, *own_w, *recv_w)
        out_specs = [block] * nsrc + [clipped(0, count)] * 2 + [whole(share)] * (2 * shards)
        out_shape = [piece] * nsrc + keep(f32) + [jax.ShapeDtypeStruct(share, bf)] * (2 * shards)
        scratch = [acc, sel, sel, sel, tall, tall, wide]
    elif which == "late":
        body, products = functools.partial(late_kernel, dims, splits), 2
        in_specs = [own_block] * 2 + [recv_block] * 2
        for low, high in zip(splits, ends):
            in_specs += [clipped(low, high - low)] * 2
        operands = (*own_w[:2], *recv_w[:2], *kept)
        out_specs, out_shape = [whole((shards,) + share)] * 2, [jax.ShapeDtypeStruct((shards,) + share, bf)] * 2
        scratch = [acc, tall, tall]
    else:
        body, products = functools.partial(middle_kernel, dims, begin), 3
        pre = pl.BlockSpec((1, total, blk), lambda r, *_: (begin + r, 0, 0))
        in_specs = [whole(tok_all.shape), own_block, recv_block] + [pre] * 2
        operands = (tok_all, own_w[2], recv_w[2], *kept)
        out_specs, out_shape = [block] * (2 * nsrc) + [clipped(0, steps)] * 2, [piece] * (2 * nsrc) + keep(bf)
        scratch = [sel, sel, sel, wide]
    flops = 2 * products * slots * steps * total * blk * blk
    return pl.pallas_call(
        body,
        grid_spec=pltpu.PrefetchScalarGridSpec(
            num_scalar_prefetch=3, grid=(steps,), in_specs=in_specs, out_specs=out_specs, scratch_shapes=scratch,
        ),
        out_shape=out_shape,
        compiler_params=pltpu.CompilerParams(vmem_limit_bytes=60 * 1024 * 1024),
        cost_estimate=pl.CostEstimate(flops=flops, bytes_accessed=40 << 20, transcendentals=0),
    )(*scalars, *operands)


def add_kernel(pairs, *refs):
    for a, b, out in zip(refs[:pairs], refs[pairs : 2 * pairs], refs[2 * pairs :]):
        out[...] = (a[...].astype(jnp.float32) + b[...].astype(jnp.float32)).astype(out.dtype)


def add_pairs(left, right):
    pairs, (near, blocks, tok, blk) = len(left), left[0].shape
    spec = pl.BlockSpec((1, blocks // 2, tok, blk), lambda i, j: (i, j, 0, 0))
    return pl.pallas_call(
        functools.partial(add_kernel, pairs),
        grid=(near, 2),
        in_specs=[spec] * (2 * pairs),
        out_specs=[spec] * pairs,
        out_shape=[jax.ShapeDtypeStruct(left[0].shape, left[0].dtype)] * pairs,
        compiler_params=pltpu.CompilerParams(vmem_limit_bytes=32 * 1024 * 1024),
    )(*left, *right)


def reduce_kernel(shards, own, other, first, *refs):
    shares, refs = refs[: shards - 1], refs[shards - 1 :]
    (out_ref, in_ref, chip, core_box, line_box, far, far_box, near, early,
     load_sem, core_send, core_recv, line_send, line_recv, far_send, far_recv, early_sem) = refs
    part, t, f = lax.axis_index("parts"), lax.axis_index("tensor"), lax.axis_index("fsdp")
    last = shards - 1
    f32, bf = jnp.float32, jnp.bfloat16
    partner = (part, t, (f // 2) * 2 + 1 - f % 2)
    across = (part, t, (f + 2) % 4)

    def to(where, src, dst, send, recv):
        return pltpu.make_async_remote_copy(
            src_ref=src, dst_ref=dst, send_sem=send, recv_sem=recv,
            device_id=where, device_id_type=pl.DeviceIdType.MESH,
        )

    barrier = pltpu.get_barrier_semaphore()
    for where in (partner, across):
        pl.semaphore_signal(barrier, inc=1, device_id=where, device_id_type=pl.DeviceIdType.MESH)

    @pl.when(t > 0)
    def _():
        pl.semaphore_signal(barrier, inc=1, device_id=(part, t - 1, f), device_id_type=pl.DeviceIdType.MESH)

    @pl.when(t < last)
    def _():
        pl.semaphore_signal(barrier, inc=1, device_id=(part, t + 1, f), device_id_type=pl.DeviceIdType.MESH)

    ends = jnp.logical_or(t == 0, t == last)

    @pl.when(ends)
    def _():
        pl.semaphore_wait(barrier, 3)

    @pl.when(jnp.logical_not(ends))
    def _():
        pl.semaphore_wait(barrier, 4)

    def place(i):
        return jnp.where(t * 2 < shards, last - i, i)

    order = [(i, x) for i in range(shards) for x in (1, 0)]
    cores, loads = {}, {}
    for i, x in order:
        d = place(i)
        cores[i, x] = to(partner, other.at[d, x], core_box.at[d, x], core_send.at[d, x], core_recv.at[d, x])
        loads[i, x] = pltpu.make_async_copy(own.at[d, x], chip.at[d, x], load_sem.at[d, x])
        cores[i, x].start()
        loads[i, x].start()
    fetch = [
        pltpu.make_async_copy(ref, early.at[k], early_sem.at[k]) for k, ref in enumerate((first,) + tuple(shares))
    ]
    for c in fetch:
        c.start()

    def line(up, d, x):
        where = (part, jnp.where(up, t + 1, t - 1), f)
        w = jnp.where(up, 0, 1)
        return to(where, chip.at[d, x], line_box.at[w, d, x], line_send.at[w, d, x], line_recv.at[w, d, x])

    def gathered(i, x):
        d = place(i)
        loads[i, x].wait()
        cores[i, x].wait_recv()
        chip[d, x] = (chip[d, x].astype(f32) + core_box[d, x].astype(f32)).astype(bf)

    def forward(up, i, x):
        d = jnp.where(up, last - i, i)
        w = jnp.where(up, 0, 1)
        fed = jnp.where(up, t > 0, t < last)

        @pl.when(jnp.where(up, t < d, t > d))
        def _():
            @pl.when(fed)
            def _():
                line(up, d, x).wait_recv()
                chip[d, x] = (chip[d, x].astype(f32) + line_box[w, d, x].astype(f32)).astype(bf)

            line(up, d, x).start()

    low = t * 2 < shards
    for i, x in order:
        gathered(i, x)

        @pl.when(jnp.where(low, t == 0, t == last))
        def _():
            forward(low, i, x)

    for i in range(shards - 1):
        for x in (1, 0):
            @pl.when(jnp.logical_not(ends))
            def _():
                forward(low, i, x)

        for x in (1, 0):
            forward(jnp.logical_not(low), i, x)

    def send_far(k):
        return to(across, far.at[k], far_box.at[k], far_send.at[k], far_recv.at[k])

    for c in fetch:
        c.wait()

    def early_sum(x):
        return sum(early[k, x].astype(f32) for k in range(shards))

    far[0] = early_sum(1).astype(bf)
    send_far(0).start()
    near[0] = early_sum(0)

    def late_sum(x):
        near[1] = chip[t, x].astype(f32)
        for up in (True, False):
            @pl.when(t > 0 if up else t < last)
            def _():
                line(jnp.bool_(up), t, x).wait_recv()
                near[1] += line_box[0 if up else 1, t, x].astype(f32)

    late_sum(1)
    far[1] = near[1].astype(bf)
    send_far(1).start()
    late_sum(0)
    blocks, blk = near.shape[1], near.shape[3]
    for k, ref in enumerate((out_ref, in_ref)):
        send_far(k).wait_recv()
        for d in range(blocks):
            ref[:, d * blk : (d + 1) * blk] = (near[k, d] + far_box[k, d].astype(f32)).astype(bf)
    for k in range(2):
        send_far(k).wait_send()
    for i, x in order:
        cores[i, x].wait_send()
    for d in range(shards):
        for x in range(2):
            @pl.when(t < d)
            def _():
                line(jnp.bool_(True), d, x).wait_send()

            @pl.when(t > d)
            def _():
                line(jnp.bool_(False), d, x).wait_send()


def reduce(own, other, shares, width):
    shards, _, blocks, tok, blk = own.shape
    bf, f32 = jnp.bfloat16, jnp.float32
    dma = lambda *a: pltpu.SemaphoreType.DMA(a)
    anywhere = pl.BlockSpec(memory_space=pl.ANY)
    unit = (blocks, tok, blk)
    pair = (shards, 2)
    return pl.pallas_call(
        functools.partial(reduce_kernel, shards),
        out_shape=[jax.ShapeDtypeStruct((tok, width), bf)] * 2,
        in_specs=[anywhere] * (2 + shards),
        out_specs=[pl.BlockSpec(memory_space=pltpu.VMEM)] * 2,
        scratch_shapes=[
            pltpu.VMEM(pair + unit, bf), pltpu.VMEM(pair + unit, bf), pltpu.VMEM((2,) + pair + unit, bf),
            pltpu.VMEM((2,) + unit, bf), pltpu.VMEM((2,) + unit, bf), pltpu.VMEM((2,) + unit, f32),
            pltpu.VMEM(pair + unit, bf),
            dma(*pair), dma(*pair), dma(*pair), dma(2, *pair), dma(2, *pair), dma(2), dma(2), dma(shards),
        ],
        compiler_params=pltpu.CompilerParams(collective_id=1, has_side_effects=True, vmem_limit_bytes=24 * 1024 * 1024),
    )(own, other, *shares)


def swap(value, flip, axis="fsdp"):
    return lax.ppermute(value, axis, [(i, i ^ flip) for i in range(lax.axis_size(axis))])


def exchanged_plan(
    tokens,
    cotangent,
    gate_values,
    gate_rows,
    gate_scale,
    up_values,
    up_rows,
    up_scale,
    down_values,
    down_cols,
    down_scale,
):
    tok, width = tokens.shape
    per_dev, local_cols, blk, _ = gate_values.shape
    count = local_cols // 4
    mine, shard = lax.axis_index("fsdp"), lax.axis_index("tensor")
    f32, bf = jnp.float32, jnp.bfloat16

    shards = lax.axis_size("tensor")
    both = jnp.stack([tokens, cotangent]).reshape(2, tok, width // blk, blk).transpose(0, 2, 1, 3)
    small = jnp.stack(
        [a.astype(f32) for a in (gate_rows, up_rows, down_cols, gate_scale, up_scale, down_scale)]
    )
    small = small.reshape(6, per_dev, 4, count).transpose(2, 0, 1, 3)
    own_w = (gate_values, up_values, down_values)
    tok_all, *recv_w, table = gather(small, both, own_w, shards)
    kept = lax.dynamic_slice_in_dim(small, mine, 1, axis=0)
    table = jnp.concatenate([kept, table]).transpose(1, 0, 2, 3).reshape(6, 4 * per_dev, count)
    table_rows = table[:3].astype(jnp.int32)
    table_scale = table[3:]
    splits = (0, (count + 1) // 2)

    def home(parts):
        result = jnp.zeros((per_dev, local_cols, blk, blk), bf)
        for begin, pieces in parts:
            for m, piece in enumerate(pieces):
                result = lax.dynamic_update_slice_in_dim(result, piece, (mine ^ m) * count + begin, axis=1)
        return result

    def send(pieces):
        return [p if m == 0 else swap(p, m) for m, p in enumerate(pieces)]

    scalars = (table_rows, table_scale, jnp.stack([mine, shard]).astype(jnp.int32))
    early = columns("early", scalars, tok_all, own_w, recv_w, (), splits)
    down_pieces, pre, own, other = early[:4], early[4:6], early[6 : 6 + shards], early[6 + shards :]
    chip = add_pairs(own, [swap(b, 1) for b in other])
    down_sent = send(down_pieces)
    chip, pre = lax.optimization_barrier((chip, pre))
    out_shares = [c if m == 0 else swap(c, m, "tensor") for m, c in enumerate(chip)]
    acts, gate_sent, up_sent = [], [], []
    for i, begin in enumerate(splits):
        middle = columns(i, scalars, tok_all, own_w, recv_w, pre, splits)
        gate_sent.append((begin, send(middle[:4])))
        up_sent.append((begin, send(middle[4:8])))
        acts += middle[8:]
        pre, acts = lax.optimization_barrier((pre, acts))
    own, other = columns("late", scalars, tok_all, own_w, recv_w, acts, splits)
    layer_out, grad_tokens = reduce(own, other, out_shares, width)
    return (layer_out, grad_tokens, home(gate_sent), home(up_sent), home([(0, down_sent)]))


def choose_plan(mesh, *args):
    fits = mesh.shape["fsdp"] == 4 and mesh.shape["parts"] == 2 and args[2].shape[0] == 2
    fits = fits and args[2].shape[1] % 4 == 0 and mesh.shape["tensor"] in (2, 4, 8)
    plan = exchanged_plan if fits else gathered_plan
    return plan(*args)


def solution(mesh):
    plan = functools.partial(choose_plan, mesh)
    in_specs = (
        P(("parts", "fsdp"), "tensor"),
        P(("parts", "fsdp"), "tensor"),
        P("fsdp", "tensor", None, None),
        P("fsdp", "tensor"),
        P("fsdp", "tensor"),
        P("fsdp", "tensor", None, None),
        P("fsdp", "tensor"),
        P("fsdp", "tensor"),
        P("fsdp", "tensor", None, None),
        P("fsdp", "tensor"),
        P("fsdp", "tensor"),
    )
    out_specs = (
        P(("parts", "fsdp"), "tensor"),
        P(("parts", "fsdp"), "tensor"),
        P(("parts", "fsdp"), "tensor", None, None),
        P(("parts", "fsdp"), "tensor", None, None),
        P(("parts", "fsdp"), "tensor", None, None),
    )
    return jax.shard_map(plan, mesh=mesh, in_specs=in_specs, out_specs=out_specs, check_vma=False)
```

```python
import functools

import jax
import jax.numpy as jnp
from jax import lax
from jax.experimental import pallas as pl
from jax.experimental.pallas import tpu as pltpu
from jax.sharding import PartitionSpec as P


def scaled_sum(products, factors):
    return jnp.sum(products * factors.astype(jnp.float32)[None, :, :, None], axis=1)


def slot_term(selected, grads, factors):
    return (
        jnp.einsum("tkra,trb->krab", selected, grads, preferred_element_type=jnp.float32)
        * factors[:, :, None, None]
    )


def gathered_plan(
    tokens,
    cotangent,
    gate_values,
    gate_rows,
    gate_scale,
    up_values,
    up_rows,
    up_scale,
    down_values,
    down_cols,
    down_scale,
):
    block_size = gate_values.shape[-1]
    token_count = tokens.shape[0]
    tensor_count = lax.axis_size("tensor")
    nblocks = tokens.shape[1] * tensor_count // block_size
    local_blocks = nblocks // tensor_count
    gathered = lax.all_gather(tokens, "tensor", axis=1, tiled=True)
    x_blocks = gathered.reshape(token_count, nblocks, block_size)
    gate_where, up_where, down_where = (
        lax.all_gather(gate_rows, "fsdp", axis=0, tiled=True),
        lax.all_gather(up_rows, "fsdp", axis=0, tiled=True),
        lax.all_gather(down_cols, "fsdp", axis=0, tiled=True),
    )
    gate_blocks, gate_factor, up_blocks, up_factor, down_blocks, down_factor = (
        lax.all_gather(gate_values, "fsdp", axis=0, tiled=True),
        lax.all_gather(gate_scale, "fsdp", axis=0, tiled=True),
        lax.all_gather(up_values, "fsdp", axis=0, tiled=True),
        lax.all_gather(up_scale, "fsdp", axis=0, tiled=True),
        lax.all_gather(down_values, "fsdp", axis=0, tiled=True),
        lax.all_gather(down_scale, "fsdp", axis=0, tiled=True),
    )
    gate_sel = x_blocks[:, gate_where]
    up_sel = x_blocks[:, up_where]
    gate_pre = scaled_sum(
        jnp.einsum("tkra,krab->tkrb", gate_sel, gate_blocks, preferred_element_type=jnp.float32),
        gate_factor,
    )
    up_pre = scaled_sum(
        jnp.einsum("tkra,krab->tkrb", up_sel, up_blocks, preferred_element_type=jnp.float32),
        up_factor,
    )
    sigmoid_gate = jax.nn.sigmoid(gate_pre)
    activated = gate_pre * sigmoid_gate
    hidden = (activated * up_pre).astype(jnp.bfloat16)
    down_float = down_factor.astype(jnp.float32)
    down_scaled = (
        jnp.einsum("trb,krbc->krtc", hidden, down_blocks, preferred_element_type=jnp.float32)
        * down_float[:, :, None, None]
    )
    out_full = (
        jnp.zeros((nblocks, token_count, block_size), jnp.float32).at[down_where].add(down_scaled)
    )
    out_part = lax.psum_scatter(
        out_full.astype(jnp.bfloat16), "tensor", scatter_dimension=0, tiled=True
    ).astype(jnp.float32)
    layer_out = (
        jnp.transpose(out_part, (1, 0, 2))
        .reshape(token_count, local_blocks * block_size)
        .astype(jnp.bfloat16)
    )
    grad_full = lax.all_gather(cotangent, "tensor", axis=1, tiled=True).reshape(
        token_count, nblocks, block_size
    )
    down_sel = grad_full[:, down_where]
    gate_float = gate_factor.astype(jnp.float32)
    up_float = up_factor.astype(jnp.float32)
    grad_hidden = scaled_sum(
        jnp.einsum("tkrc,krbc->tkrb", down_sel, down_blocks, preferred_element_type=jnp.float32),
        down_factor,
    )
    grad_down = lax.psum_scatter(
        (
            jnp.einsum("trb,tkrc->krbc", hidden, down_sel, preferred_element_type=jnp.float32)
            * down_float[:, :, None, None]
        ).astype(jnp.bfloat16),
        "fsdp",
        scatter_dimension=0,
        tiled=True,
    )
    grad_gate_act = (
        grad_hidden * up_pre * sigmoid_gate * (1.0 + gate_pre * (1.0 - sigmoid_gate))
    ).astype(jnp.bfloat16)
    grad_up_act = (grad_hidden * activated).astype(jnp.bfloat16)
    grad_gate = lax.psum_scatter(
        slot_term(gate_sel, grad_gate_act, gate_float).astype(jnp.bfloat16),
        "fsdp",
        scatter_dimension=0,
        tiled=True,
    )
    grad_up = lax.psum_scatter(
        slot_term(up_sel, grad_up_act, up_float).astype(jnp.bfloat16),
        "fsdp",
        scatter_dimension=0,
        tiled=True,
    )
    back_gate = (
        jnp.einsum("trb,krab->krta", grad_gate_act, gate_blocks, preferred_element_type=jnp.float32)
        * gate_float[:, :, None, None]
    )
    back_up = (
        jnp.einsum("trb,krab->krta", grad_up_act, up_blocks, preferred_element_type=jnp.float32)
        * up_float[:, :, None, None]
    )
    in_full = (
        jnp.zeros((nblocks, token_count, block_size), jnp.float32)
        .at[gate_where]
        .add(back_gate)
        .at[up_where]
        .add(back_up)
    )
    in_part = lax.psum_scatter(
        in_full.astype(jnp.bfloat16), "tensor", scatter_dimension=0, tiled=True
    ).astype(jnp.float32)
    grad_tokens = (
        jnp.transpose(in_part, (1, 0, 2))
        .reshape(token_count, local_blocks * block_size)
        .astype(jnp.bfloat16)
    )
    return (layer_out, grad_tokens, grad_gate, grad_up, grad_down)


def gather_kernel(shards, tokens, cotangent, *refs):
    rows, factors, (wg, wu, wd), refs = refs[:3], refs[3:6], refs[6:9], refs[9:]
    tok_all, rg, ru, rd, row_table, factor_table, spot, both, *sems = refs
    (z_send, z_recv, c_send, c_recv, x_send, x_recv, w_send, w_recv, y_send, y_recv, n_send, n_recv, s_send, s_recv, here) = sems
    part, t, f = lax.axis_index("parts"), lax.axis_index("tensor"), lax.axis_index("fsdp")
    flip = [f, (f // 2) * 2 + 1 - f % 2, (f + 2) % 4, ((f + 2) % 4 // 2) * 2 + 1 - f % 2]
    count = rg.shape[2]
    last = shards - 1
    weights = ((wg, rg), (wu, ru), (wd, rd))

    def to(where, src, dst, send, recv):
        return pltpu.make_async_remote_copy(
            src_ref=src, dst_ref=dst, send_sem=send, recv_sem=recv,
            device_id=where, device_id_type=pl.DeviceIdType.MESH,
        )

    def across(m):
        return (part, t, flip[m])

    over = (1 - part, t, f)
    ups = ((part, t + 1, f), (part, t - 1, f))
    more = (t < last, t > 0)
    spot[0], spot[1] = f, t
    blk = both.shape[3]
    for which, ref in enumerate((tokens, cotangent)):
        for d in range(both.shape[1]):
            both[which, d] = ref[:, d * blk : (d + 1) * blk]
    for array in range(3):
        row_table[0, array] = rows[array][...]
        factor_table[0, array] = factors[array][...].astype(jnp.float32)

    barrier = pltpu.get_barrier_semaphore()
    for m in (1, 2, 3):
        pl.semaphore_signal(barrier, inc=1, device_id=across(m), device_id_type=pl.DeviceIdType.MESH)
    pl.semaphore_signal(barrier, inc=1, device_id=over, device_id_type=pl.DeviceIdType.MESH)
    for way in range(2):
        @pl.when(more[way])
        def _():
            pl.semaphore_signal(barrier, inc=1, device_id=ups[way], device_id_type=pl.DeviceIdType.MESH)
    ends = jnp.logical_or(t == 0, t == last)

    @pl.when(ends)
    def _():
        pl.semaphore_wait(barrier, 5)

    @pl.when(jnp.logical_not(ends))
    def _():
        pl.semaphore_wait(barrier, 6)

    def z_copy(way, src, x, own=False):
        source = both if own else tok_all.at[0, src, x]
        return to(ups[way], source, tok_all.at[0, src, x], z_send.at[way, src, x], z_recv.at[way, src, x])

    def c_copy(src, x, own=False):
        source = both if own else tok_all.at[0, src, x]
        return to(across(1), source, tok_all.at[1, src, x], c_send.at[src, x], c_recv.at[src, x])

    x_copy = to(across(2), both, tok_all.at[0, t, 1], x_send, x_recv)
    keep = pltpu.make_async_copy(both, tok_all.at[0, t, 0], here)
    x_copy.start()
    for way in range(2):
        @pl.when(more[way])
        def _():
            z_copy(way, t, 0, True).start()
    tables = [
        to(across(m), table.at[0], table.at[m], s_send.at[i, m - 1], s_recv.at[i, m - 1])
        for i, table in enumerate((row_table, factor_table))
        for m in (1, 2, 3)
    ]
    for c in tables:
        c.start()
    c_copy(t, 0, True).start()
    w_copies, y_copies, y_waits, n_copies = [], [], [], []
    for w, r in weights:
        for m in (2, 3):
            j = len(w_copies)
            w_copies.append(to(across(m), w.at[part, pl.ds(flip[m] * count, count)], r.at[m - 1, part], w_send.at[j], w_recv.at[j]))
            y_copies.append(to(over, r.at[m - 1, part], r.at[m - 1, part], y_send.at[j], y_recv.at[j]))
            y_waits.append(to(over, r.at[m - 1, part], r.at[m - 1, 1 - part], y_send.at[j], y_recv.at[j]))
        for k in range(2):
            j = len(n_copies)
            n_copies.append(to(across(1), w.at[k, pl.ds(flip[1] * count, count)], r.at[0, k], n_send.at[j], n_recv.at[j]))
    for c in w_copies:
        c.start()
    for c in n_copies:
        c.start()
    keep.start()

    x_copy.wait_recv()
    for way in range(2):
        @pl.when(more[way])
        def _():
            z_copy(way, t, 1).start()
    c_copy(t, 1).start()

    def arrive(step, x):
        for way in range(2):
            src = t - step if way == 0 else t + step

            @pl.when(src >= 0 if way == 0 else src <= last)
            def _():
                z_copy(way, src, x).wait_recv()

                @pl.when(more[way])
                def _():
                    z_copy(way, src, x).start()

                c_copy(src, x).start()

    def relay(j):
        w_copies[j].wait_recv()
        y_copies[j].start()

    order = [(s, x) for s in range(1, shards) for x in range(2)]
    done = 0
    for i, (s, x) in enumerate(order):
        arrive(s, x)
        while done < len(w_copies) and done < 2 * i + 1:
            relay(done)
            done += 1
    while done < len(w_copies):
        relay(done)
        done += 1

    for way in range(2):
        for s in range(shards):
            src = t - s if way == 0 else t + s

            @pl.when(jnp.logical_and(src >= 0 if way == 0 else src <= last, more[way]))
            def _():
                for x in range(2):
                    z_copy(way, src, x, s == 0 and x == 0).wait_send()
    for src in range(shards):
        for x in range(2):
            c_copy(src, x).wait_send()
            c_copy(src, x).wait_recv()
    for c in tables + n_copies:
        c.wait_send()
        c.wait_recv()
    x_copy.wait_send()
    for c in w_copies + y_copies:
        c.wait_send()
    for c in y_waits:
        c.wait_recv()
    keep.wait()


def gather(tokens, cotangent, rows, factors, weights, shards):
    per_dev, local_cols, blk, _ = weights[0].shape
    count = local_cols // 4
    tok, width = tokens.shape
    bf = jnp.bfloat16
    dma = lambda *a: pltpu.SemaphoreType.DMA(a)
    received = jax.ShapeDtypeStruct((3, per_dev, count, blk, blk), bf)
    anywhere, local = pl.BlockSpec(memory_space=pl.ANY), pl.BlockSpec(memory_space=pltpu.VMEM)
    both = (2, width // blk, tok, blk)
    table = (4, 3, per_dev, local_cols)
    z = (2, shards, 2)
    c = (shards, 2)
    one = pltpu.SemaphoreType.DMA
    return pl.pallas_call(
        functools.partial(gather_kernel, shards),
        out_shape=[
            jax.ShapeDtypeStruct((2, shards, 2) + both, bf),
            received, received, received,
            jax.ShapeDtypeStruct(table, jnp.int32),
            jax.ShapeDtypeStruct(table, jnp.float32),
            jax.ShapeDtypeStruct((2,), jnp.int32),
        ],
        in_specs=[local] * 8 + [anywhere] * 3,
        out_specs=[anywhere] * 4 + [local] * 2 + [pl.BlockSpec(memory_space=pltpu.SMEM)],
        scratch_shapes=[
            pltpu.VMEM(both, bf),
            dma(*z), dma(*z), dma(*c), dma(*c), one, one, dma(6), dma(6), dma(6), dma(6), dma(6), dma(6), dma(2, 3), dma(2, 3), one,
        ],
        compiler_params=pltpu.CompilerParams(collective_id=0, has_side_effects=True),
    )(tokens, cotangent, *rows, *factors, *weights)


NN = (((1,), (0,)), ((), ()))
NT = (((1,), (1,)), ((), ()))
dot = functools.partial(lax.dot_general, preferred_element_type=jnp.float32)


def entry(table_ref, array, slot, r):
    per_dev = table_ref.shape[2]
    return table_ref[slot // per_dev, array, slot % per_dev, r]


def load(rows_ref, tok_ref, tok, which, array, slot, r, sel):
    per_shard, blk = tok_ref.shape[4], tok_ref.shape[6]
    place = entry(rows_ref, array, slot, r)
    shard, block = place // per_shard, place % per_shard
    for c in range(2):
        for x in range(2):
            q = c * 2 + x
            sel[q * tok : (q + 1) * tok, slot * blk : (slot + 1) * blk] = tok_ref[c, shard, x, which, block]


def scaled(scale_ref, own, recv, array, slot, r):
    per_dev = own.shape[0]
    src, sub = slot // per_dev, slot % per_dev
    value = recv[src - 1, sub, 0] if src else own[sub, 0]
    return (value.astype(jnp.float32) * entry(scale_ref, array, slot, r)).astype(jnp.bfloat16)


def accumulate(rows_ref, acc, array, slots, r, blk, product):
    for slot in range(slots):
        acc[entry(rows_ref, array, slot, r)] += product[:, slot * blk : (slot + 1) * blk]


def clear(acc):
    @pl.when(pl.program_id(0) == 0)
    def _():
        acc[...] = jnp.zeros_like(acc)


def flush(shard, acc, tok, own, other):
    per_shard = own[0].shape[1]

    @pl.when(pl.program_id(0) == pl.num_programs(0) - 1)
    def _():
        for m in range(len(own)):
            first = (shard ^ m) * per_shard
            for c, ref in enumerate((own[m], other[m])):
                for x in range(2):
                    q = c * 2 + x

                    @pl.loop(0, per_shard)
                    def _(d):
                        ref[x, d] = acc[first + d, q * tok : (q + 1) * tok, :].astype(jnp.bfloat16)


def early_kernel(dims, rows_ref, scale_ref, place_ref, tok_ref, *refs):
    slots, per_dev, tok, blk, shards = dims
    nsrc = slots // per_dev
    own_w, recv_w, refs = refs[:3], refs[3:6], refs[6:]
    grads, (gate_pre_ref, up_pre_ref), refs = refs[:nsrc], refs[nsrc : nsrc + 2], refs[nsrc + 2 :]
    own, other, scratch = refs[:shards], refs[shards : 2 * shards], refs[2 * shards :]
    acc, gate_sel, up_sel, down_sel, gate_w, up_w, down_w = scratch
    r = place_ref[0] * pl.num_programs(0) + pl.program_id(0)
    clear(acc)
    for slot in range(slots):
        span = slice(slot * blk, (slot + 1) * blk)
        load(rows_ref, tok_ref, tok, 0, 0, slot, r, gate_sel)
        load(rows_ref, tok_ref, tok, 0, 1, slot, r, up_sel)
        load(rows_ref, tok_ref, tok, 1, 2, slot, r, down_sel)
        gate_w[span, :] = scaled(scale_ref, own_w[0], recv_w[0], 0, slot, r)
        up_w[span, :] = scaled(scale_ref, own_w[1], recv_w[1], 1, slot, r)
        down_w[:, span] = scaled(scale_ref, own_w[2], recv_w[2], 2, slot, r)
    gate_pre = dot(gate_sel[...], gate_w[...], NN)
    up_pre = dot(up_sel[...], up_w[...], NN)
    gate_pre_ref[0], up_pre_ref[0] = gate_pre, up_pre
    hidden = (gate_pre * jax.nn.sigmoid(gate_pre) * up_pre).astype(jnp.bfloat16)
    down = dot(hidden.T, down_sel[...], NN)
    for slot in range(slots):
        src, sub = slot // per_dev, slot % per_dev
        g = down[:, slot * blk : (slot + 1) * blk] * entry(scale_ref, 2, slot, r)
        grads[src][sub, 0] = g.astype(jnp.bfloat16)
    accumulate(rows_ref, acc, 2, slots, r, blk, dot(hidden, down_w[...], NN))
    flush(place_ref[1], acc, tok, own, other)


def middle_kernel(dims, rows_ref, scale_ref, place_ref, tok_ref, own_w, recv_w, gate_pre_ref, up_pre_ref, *refs):
    slots, per_dev, tok, blk, _ = dims
    nsrc = slots // per_dev
    grads, (gate_act_ref, up_act_ref), scratch = (refs[:nsrc], refs[nsrc : 2 * nsrc]), refs[2 * nsrc : 2 * nsrc + 2], refs[2 * nsrc + 2 :]
    gate_sel, up_sel, down_sel, down_w = scratch
    r = place_ref[0] * pl.num_programs(0) + pl.program_id(0)
    for slot in range(slots):
        load(rows_ref, tok_ref, tok, 0, 0, slot, r, gate_sel)
        load(rows_ref, tok_ref, tok, 0, 1, slot, r, up_sel)
        load(rows_ref, tok_ref, tok, 1, 2, slot, r, down_sel)
        down_w[:, slot * blk : (slot + 1) * blk] = scaled(scale_ref, own_w, recv_w, 2, slot, r)
    gate_pre, up_pre = gate_pre_ref[0], up_pre_ref[0]
    grad_hidden = dot(down_sel[...], down_w[...], NT)
    sig = jax.nn.sigmoid(gate_pre)
    act = gate_pre * sig
    gate_act = (grad_hidden * up_pre * sig * (1.0 + gate_pre * (1.0 - sig))).astype(jnp.bfloat16)
    up_act = (grad_hidden * act).astype(jnp.bfloat16)
    gate_act_ref[0], up_act_ref[0] = gate_act, up_act
    for slot in range(slots):
        span = slice(slot * blk, (slot + 1) * blk)
        src, sub = slot // per_dev, slot % per_dev
        g = dot(gate_sel[:, span].T, gate_act, NN) * entry(scale_ref, 0, slot, r)
        grads[0][src][sub, 0] = g.astype(jnp.bfloat16)
        g = dot(up_sel[:, span].T, up_act, NN) * entry(scale_ref, 1, slot, r)
        grads[1][src][sub, 0] = g.astype(jnp.bfloat16)


def late_kernel(dims, rows_ref, scale_ref, place_ref, *refs):
    slots, per_dev, tok, blk, shards = dims
    nsrc = slots // per_dev
    own_w, recv_w, (gate_act_ref, up_act_ref), pieces, refs = refs[:2], refs[2:4], refs[4:6], refs[6 : 6 + nsrc], refs[6 + nsrc :]
    own_ref, other_ref, placed_ref, acc, gate_w, up_w = refs
    own, other = [own_ref.at[d] for d in range(shards)], [other_ref.at[d] for d in range(shards)]
    r = place_ref[0] * pl.num_programs(0) + pl.program_id(0)
    clear(acc)
    for m, piece in enumerate(pieces):
        placed_ref[:, place_ref[0] ^ m, 0] = piece[:, 0]
    for slot in range(slots):
        span = slice(slot * blk, (slot + 1) * blk)
        gate_w[span, :] = scaled(scale_ref, own_w[0], recv_w[0], 0, slot, r)
        up_w[span, :] = scaled(scale_ref, own_w[1], recv_w[1], 1, slot, r)
    accumulate(rows_ref, acc, 0, slots, r, blk, dot(gate_act_ref[0], gate_w[...], NT))
    accumulate(rows_ref, acc, 1, slots, r, blk, dot(up_act_ref[0], up_w[...], NT))
    flush(0, acc, tok, own, other)


def columns(which, scalars, tok_all, own_w, recv_w, kept):
    nsrc = 1 + recv_w[0].shape[0]
    _, per_dev, count, blk, _ = recv_w[0].shape
    _, shards, _, _, per_shard, tok, _ = tok_all.shape
    nblk = shards * per_shard
    slots = per_dev * nsrc
    total = 4 * tok
    bf, f32 = jnp.bfloat16, jnp.float32
    whole = lambda a: pl.BlockSpec(a, lambda r, *_: (0,) * len(a), pipeline_mode=pl.Buffered(1))
    own_block = pl.BlockSpec((per_dev, 1, blk, blk), lambda r, rows, scale, at: (0, at[0] * count + r, 0, 0))
    recv_block = pl.BlockSpec((nsrc - 1, per_dev, 1, blk, blk), lambda r, *_: (0, 0, r, 0, 0))
    block = pl.BlockSpec((per_dev, 1, blk, blk), lambda r, *_: (0, r, 0, 0))
    piece = jax.ShapeDtypeStruct((per_dev, count, blk, blk), bf)
    kept_block = [pl.BlockSpec((1, total, blk), lambda r, *_: (r, 0, 0))] * 2
    keep = lambda kind: [jax.ShapeDtypeStruct((count, total, blk), kind)] * 2
    share = (2, per_shard, tok, blk)
    acc = pltpu.VMEM((nblk, total, blk), f32)
    sel = pltpu.VMEM((total, slots * blk), bf)
    tall, wide = pltpu.VMEM((slots * blk, blk), bf), pltpu.VMEM((blk, slots * blk), bf)
    dims = (slots, per_dev, tok, blk, shards)
    if which == "early":
        body, products = functools.partial(early_kernel, dims), 4
        in_specs = [whole(tok_all.shape)] + [own_block] * 3 + [recv_block] * 3
        operands = (tok_all, *own_w, *recv_w)
        out_specs = [block] * nsrc + kept_block + [whole(share)] * (2 * shards)
        out_shape = [piece] * nsrc + keep(f32) + [jax.ShapeDtypeStruct(share, bf)] * (2 * shards)
        scratch = [acc, sel, sel, sel, tall, tall, wide]
    elif which == "late":
        body, products = functools.partial(late_kernel, dims), 2
        in_specs = [own_block] * 2 + [recv_block] * 2 + kept_block + [block] * nsrc
        operands = (*own_w[:2], *recv_w[:2], *kept)
        placed = pl.BlockSpec((per_dev, nsrc, 1, blk, blk), lambda r, *_: (0, 0, r, 0, 0))
        out_specs = [whole((shards,) + share)] * 2 + [placed]
        out_shape = [jax.ShapeDtypeStruct((shards,) + share, bf)] * 2
        out_shape += [jax.ShapeDtypeStruct((per_dev, nsrc, count, blk, blk), bf)]
        scratch = [acc, tall, tall]
    else:
        body, products = functools.partial(middle_kernel, dims), 3
        in_specs = [whole(tok_all.shape), own_block, recv_block] + kept_block
        operands = (tok_all, own_w[2], recv_w[2], *kept)
        out_specs, out_shape = [block] * (2 * nsrc) + kept_block, [piece] * (2 * nsrc) + keep(bf)
        scratch = [sel, sel, sel, wide]
    flops = 2 * products * slots * count * total * blk * blk
    return pl.pallas_call(
        body,
        grid_spec=pltpu.PrefetchScalarGridSpec(
            num_scalar_prefetch=3, grid=(count,), in_specs=in_specs, out_specs=out_specs, scratch_shapes=scratch,
        ),
        out_shape=out_shape,
        compiler_params=pltpu.CompilerParams(vmem_limit_bytes=64_600_000 if which == "late" else 60 * 1024 * 1024),
        cost_estimate=pl.CostEstimate(flops=flops, bytes_accessed=40 << 20, transcendentals=0),
    )(*scalars, *operands)


def add_kernel(pairs, *refs):
    left, right, out, (held, load_sem, store_sem) = refs[:pairs], refs[pairs : 2 * pairs], refs[2 * pairs : 3 * pairs], refs[3 * pairs :]
    loads = [pltpu.make_async_copy(a, held.at[0, m], load_sem.at[m]) for m, a in enumerate(left)]
    stores = [pltpu.make_async_copy(held.at[1, m], c, store_sem.at[m]) for m, c in enumerate(out)]
    for c in loads:
        c.start()
    for m in reversed(range(pairs)):
        loads[m].wait()
        held[1, m] = (held[0, m].astype(jnp.float32) + right[m][...].astype(jnp.float32)).astype(held.dtype)
        stores[m].start()
    for c in stores:
        c.wait()


def add_pairs(left, right):
    pairs, unit = len(left), left[0]
    stay, local = pl.BlockSpec(memory_space=pltpu.HBM), pl.BlockSpec(memory_space=pltpu.VMEM)
    dma = pltpu.SemaphoreType.DMA((pairs,))
    return pl.pallas_call(
        functools.partial(add_kernel, pairs),
        in_specs=[stay] * pairs + [local] * pairs,
        out_specs=[stay] * pairs,
        out_shape=[jax.ShapeDtypeStruct(unit.shape, unit.dtype)] * pairs,
        scratch_shapes=[pltpu.VMEM((2, pairs) + unit.shape, unit.dtype), dma, dma],
        compiler_params=pltpu.CompilerParams(vmem_limit_bytes=64_600_000),
    )(*left, *right)


def reduce_kernel(shards, own, other, first, *refs):
    shares, refs = refs[: shards - 1], refs[shards - 1 :]
    (out_ref, in_ref, chip, core_box, line_box, far, far_box, near, early,
     load_sem, core_send, core_recv, line_send, line_recv, far_send, far_recv, early_sem) = refs
    part, t, f = lax.axis_index("parts"), lax.axis_index("tensor"), lax.axis_index("fsdp")
    last = shards - 1
    f32, bf = jnp.float32, jnp.bfloat16
    partner = (part, t, (f // 2) * 2 + 1 - f % 2)
    across = (part, t, (f + 2) % 4)

    def to(where, src, dst, send, recv):
        return pltpu.make_async_remote_copy(
            src_ref=src, dst_ref=dst, send_sem=send, recv_sem=recv,
            device_id=where, device_id_type=pl.DeviceIdType.MESH,
        )

    barrier = pltpu.get_barrier_semaphore()
    for where in (partner, across):
        pl.semaphore_signal(barrier, inc=1, device_id=where, device_id_type=pl.DeviceIdType.MESH)

    @pl.when(t > 0)
    def _():
        pl.semaphore_signal(barrier, inc=1, device_id=(part, t - 1, f), device_id_type=pl.DeviceIdType.MESH)

    @pl.when(t < last)
    def _():
        pl.semaphore_signal(barrier, inc=1, device_id=(part, t + 1, f), device_id_type=pl.DeviceIdType.MESH)

    ends = jnp.logical_or(t == 0, t == last)

    @pl.when(ends)
    def _():
        pl.semaphore_wait(barrier, 3)

    @pl.when(jnp.logical_not(ends))
    def _():
        pl.semaphore_wait(barrier, 4)

    def place(i):
        return jnp.where(t * 2 < shards, last - i, i)

    order = [(i, x) for i in range(shards) for x in (1, 0)]
    cores, loads = {}, {}
    for i, x in order:
        d = place(i)
        cores[i, x] = to(partner, other.at[d, x], core_box.at[d, x], core_send.at[d, x], core_recv.at[d, x])
        loads[i, x] = pltpu.make_async_copy(own.at[d, x], chip.at[d, x], load_sem.at[d, x])
        cores[i, x].start()
        loads[i, x].start()
    fetch = [
        pltpu.make_async_copy(ref, early.at[k], early_sem.at[k]) for k, ref in enumerate((first,) + tuple(shares))
    ]
    for c in fetch:
        c.start()

    def line(up, d, x):
        where = (part, jnp.where(up, t + 1, t - 1), f)
        w = jnp.where(up, 0, 1)
        return to(where, chip.at[d, x], line_box.at[w, d, x], line_send.at[w, d, x], line_recv.at[w, d, x])

    def gathered(i, x):
        d = place(i)
        loads[i, x].wait()
        cores[i, x].wait_recv()
        chip[d, x] = (chip[d, x].astype(f32) + core_box[d, x].astype(f32)).astype(bf)

    def forward(up, i, x):
        d = jnp.where(up, last - i, i)
        w = jnp.where(up, 0, 1)
        fed = jnp.where(up, t > 0, t < last)

        @pl.when(jnp.where(up, t < d, t > d))
        def _():
            @pl.when(fed)
            def _():
                line(up, d, x).wait_recv()
                chip[d, x] = (chip[d, x].astype(f32) + line_box[w, d, x].astype(f32)).astype(bf)

            line(up, d, x).start()

    low = t * 2 < shards
    for i, x in order:
        gathered(i, x)

        @pl.when(jnp.where(low, t == 0, t == last))
        def _():
            forward(low, i, x)

    for i in range(shards - 1):
        for x in (1, 0):
            @pl.when(jnp.logical_not(ends))
            def _():
                forward(low, i, x)

        for x in (1, 0):
            forward(jnp.logical_not(low), i, x)

    def send_far(k):
        return to(across, far.at[k], far_box.at[k], far_send.at[k], far_recv.at[k])

    for c in fetch:
        c.wait()

    def early_sum(x):
        return sum(early[k, x].astype(f32) for k in range(shards))

    far[0] = early_sum(1).astype(bf)
    send_far(0).start()
    near[0] = early_sum(0)

    def late_sum(x):
        near[1] = chip[t, x].astype(f32)
        for up in (True, False):
            @pl.when(t > 0 if up else t < last)
            def _():
                line(jnp.bool_(up), t, x).wait_recv()
                near[1] += line_box[0 if up else 1, t, x].astype(f32)

    late_sum(1)
    far[1] = near[1].astype(bf)
    send_far(1).start()
    late_sum(0)
    blocks, blk = near.shape[1], near.shape[3]
    for k, ref in enumerate((out_ref, in_ref)):
        send_far(k).wait_recv()
        for d in range(blocks):
            ref[:, d * blk : (d + 1) * blk] = (near[k, d] + far_box[k, d].astype(f32)).astype(bf)
    for k in range(2):
        send_far(k).wait_send()
    for i, x in order:
        cores[i, x].wait_send()
    for d in range(shards):
        for x in range(2):
            @pl.when(t < d)
            def _():
                line(jnp.bool_(True), d, x).wait_send()

            @pl.when(t > d)
            def _():
                line(jnp.bool_(False), d, x).wait_send()


def reduce(own, other, shares, width):
    shards, _, blocks, tok, blk = own.shape
    bf, f32 = jnp.bfloat16, jnp.float32
    dma = lambda *a: pltpu.SemaphoreType.DMA(a)
    anywhere = pl.BlockSpec(memory_space=pl.ANY)
    unit = (blocks, tok, blk)
    pair = (shards, 2)
    return pl.pallas_call(
        functools.partial(reduce_kernel, shards),
        out_shape=[jax.ShapeDtypeStruct((tok, width), bf)] * 2,
        in_specs=[anywhere] * (2 + shards),
        out_specs=[pl.BlockSpec(memory_space=pltpu.VMEM)] * 2,
        scratch_shapes=[
            pltpu.VMEM(pair + unit, bf), pltpu.VMEM(pair + unit, bf), pltpu.VMEM((2,) + pair + unit, bf),
            pltpu.VMEM((2,) + unit, bf), pltpu.VMEM((2,) + unit, bf), pltpu.VMEM((2,) + unit, f32),
            pltpu.VMEM(pair + unit, bf),
            dma(*pair), dma(*pair), dma(*pair), dma(2, *pair), dma(2, *pair), dma(2), dma(2), dma(shards),
        ],
        compiler_params=pltpu.CompilerParams(collective_id=1, has_side_effects=True, vmem_limit_bytes=66_400_000),
    )(own, other, *shares)


def home_kernel(arrays, place_ref, *refs):
    nsrc = (len(refs) - 3) // arrays - 1
    pieces, placed, (held, load_sem, store_sem) = refs[: arrays * nsrc], refs[arrays * nsrc : -3], refs[-3:]
    count = held.shape[2]
    loads, stores = [], []
    for j, piece in enumerate(pieces):
        array, m = j // nsrc, j % nsrc
        for sub in range(piece.shape[0]):
            column = (place_ref[0] ^ m) * count
            loads.append(pltpu.make_async_copy(piece.at[sub], held.at[j, sub], load_sem.at[j, sub]))
            stores.append(
                pltpu.make_async_copy(held.at[j, sub], placed[array].at[sub, pl.ds(column, count)], store_sem.at[j, sub])
            )
    for c in loads:
        c.start()
    for a, b in zip(loads, stores):
        a.wait()
        b.start()
    for c in stores:
        c.wait()


def home(place, sent):
    arrays, nsrc = len(sent), len(sent[0])
    per_dev, count, blk, _ = sent[0][0].shape
    anywhere = pl.BlockSpec(memory_space=pl.ANY)
    shape = jax.ShapeDtypeStruct((per_dev, nsrc * count, blk, blk), sent[0][0].dtype)
    held = (arrays * nsrc, per_dev)
    return pl.pallas_call(
        functools.partial(home_kernel, arrays),
        grid_spec=pltpu.PrefetchScalarGridSpec(
            num_scalar_prefetch=1, grid=(1,),
            in_specs=[anywhere] * (arrays * nsrc), out_specs=[anywhere] * arrays,
            scratch_shapes=[
                pltpu.VMEM(held + (count, blk, blk), sent[0][0].dtype), pltpu.SemaphoreType.DMA(held), pltpu.SemaphoreType.DMA(held),
            ],
        ),
        out_shape=[shape] * arrays,
        compiler_params=pltpu.CompilerParams(vmem_limit_bytes=66_400_000),
    )(place, *[piece for pieces in sent for piece in pieces])


def swap(value, flip, axis="fsdp"):
    return lax.ppermute(value, axis, [(i, i ^ flip) for i in range(lax.axis_size(axis))])


def exchanged_plan(
    tokens,
    cotangent,
    gate_values,
    gate_rows,
    gate_scale,
    up_values,
    up_rows,
    up_scale,
    down_values,
    down_cols,
    down_scale,
):
    _, width = tokens.shape
    shards = lax.axis_size("tensor")
    own_w = (gate_values, up_values, down_values)
    rows, factors = (gate_rows, up_rows, down_cols), (gate_scale, up_scale, down_scale)
    tok_all, *recv_w, row_table, factor_table, place = gather(tokens, cotangent, rows, factors, own_w, shards)
    scalars = (row_table, factor_table, place)

    def send(pieces):
        return [p if m == 0 else swap(p, m) for m, p in enumerate(pieces)]

    early = columns("early", scalars, tok_all, own_w, recv_w, ())
    down_pieces, pre, own, other = early[:4], early[4:6], early[6 : 6 + shards], early[6 + shards :]
    chip = add_pairs(own, [swap(b, 1) for b in other])
    down_sent = send(down_pieces)
    chip, pre = lax.optimization_barrier((chip, pre))
    out_shares = [c if m == 0 else swap(c, m, "tensor") for m, c in enumerate(chip)]
    middle = columns("middle", scalars, tok_all, own_w, recv_w, pre)
    gate_sent, up_sent = send(middle[:4]), send(middle[4:8])
    own, other, grad_down = columns("late", scalars, tok_all, own_w, recv_w, (*middle[8:], *down_sent))
    layer_out, grad_tokens = reduce(own, other, out_shares, width)
    grad_gate, grad_up = home(place, (gate_sent, up_sent))
    return (layer_out, grad_tokens, grad_gate, grad_up, grad_down.reshape(gate_values.shape))


def choose_plan(mesh, *args):
    fits = mesh.shape["fsdp"] == 4 and mesh.shape["parts"] == 2 and args[2].shape[0] == 2
    fits = fits and args[2].shape[1] % 4 == 0 and mesh.shape["tensor"] in (2, 4, 8)
    plan = exchanged_plan if fits else gathered_plan
    return plan(*args)


def solution(mesh):
    plan = functools.partial(choose_plan, mesh)
    in_specs = (
        P(("parts", "fsdp"), "tensor"),
        P(("parts", "fsdp"), "tensor"),
        P("fsdp", "tensor", None, None),
        P("fsdp", "tensor"),
        P("fsdp", "tensor"),
        P("fsdp", "tensor", None, None),
        P("fsdp", "tensor"),
        P("fsdp", "tensor"),
        P("fsdp", "tensor", None, None),
        P("fsdp", "tensor"),
        P("fsdp", "tensor"),
    )
    out_specs = (
        P(("parts", "fsdp"), "tensor"),
        P(("parts", "fsdp"), "tensor"),
        P(("parts", "fsdp"), "tensor", None, None),
        P(("parts", "fsdp"), "tensor", None, None),
        P(("parts", "fsdp"), "tensor", None, None),
    )
    return jax.shard_map(plan, mesh=mesh, in_specs=in_specs, out_specs=out_specs, check_vma=False)
```

```python
import functools

import jax
import jax.numpy as jnp
from jax import lax
from jax.experimental import pallas as pl
from jax.experimental.pallas import tpu as pltpu
from jax.sharding import PartitionSpec as P


def scaled_sum(products, factors):
    return jnp.sum(products * factors.astype(jnp.float32)[None, :, :, None], axis=1)


def slot_term(selected, grads, factors):
    return (
        jnp.einsum("tkra,trb->krab", selected, grads, preferred_element_type=jnp.float32)
        * factors[:, :, None, None]
    )


def gathered_plan(
    tokens,
    cotangent,
    gate_values,
    gate_rows,
    gate_scale,
    up_values,
    up_rows,
    up_scale,
    down_values,
    down_cols,
    down_scale,
):
    block_size = gate_values.shape[-1]
    token_count = tokens.shape[0]
    tensor_count = lax.axis_size("tensor")
    nblocks = tokens.shape[1] * tensor_count // block_size
    local_blocks = nblocks // tensor_count
    gathered = lax.all_gather(tokens, "tensor", axis=1, tiled=True)
    x_blocks = gathered.reshape(token_count, nblocks, block_size)
    gate_where, up_where, down_where = (
        lax.all_gather(gate_rows, "fsdp", axis=0, tiled=True),
        lax.all_gather(up_rows, "fsdp", axis=0, tiled=True),
        lax.all_gather(down_cols, "fsdp", axis=0, tiled=True),
    )
    gate_blocks, gate_factor, up_blocks, up_factor, down_blocks, down_factor = (
        lax.all_gather(gate_values, "fsdp", axis=0, tiled=True),
        lax.all_gather(gate_scale, "fsdp", axis=0, tiled=True),
        lax.all_gather(up_values, "fsdp", axis=0, tiled=True),
        lax.all_gather(up_scale, "fsdp", axis=0, tiled=True),
        lax.all_gather(down_values, "fsdp", axis=0, tiled=True),
        lax.all_gather(down_scale, "fsdp", axis=0, tiled=True),
    )
    gate_sel = x_blocks[:, gate_where]
    up_sel = x_blocks[:, up_where]
    gate_pre = scaled_sum(
        jnp.einsum("tkra,krab->tkrb", gate_sel, gate_blocks, preferred_element_type=jnp.float32),
        gate_factor,
    )
    up_pre = scaled_sum(
        jnp.einsum("tkra,krab->tkrb", up_sel, up_blocks, preferred_element_type=jnp.float32),
        up_factor,
    )
    sigmoid_gate = jax.nn.sigmoid(gate_pre)
    activated = gate_pre * sigmoid_gate
    hidden = (activated * up_pre).astype(jnp.bfloat16)
    down_float = down_factor.astype(jnp.float32)
    down_scaled = (
        jnp.einsum("trb,krbc->krtc", hidden, down_blocks, preferred_element_type=jnp.float32)
        * down_float[:, :, None, None]
    )
    out_full = (
        jnp.zeros((nblocks, token_count, block_size), jnp.float32).at[down_where].add(down_scaled)
    )
    out_part = lax.psum_scatter(
        out_full.astype(jnp.bfloat16), "tensor", scatter_dimension=0, tiled=True
    ).astype(jnp.float32)
    layer_out = (
        jnp.transpose(out_part, (1, 0, 2))
        .reshape(token_count, local_blocks * block_size)
        .astype(jnp.bfloat16)
    )
    grad_full = lax.all_gather(cotangent, "tensor", axis=1, tiled=True).reshape(
        token_count, nblocks, block_size
    )
    down_sel = grad_full[:, down_where]
    gate_float = gate_factor.astype(jnp.float32)
    up_float = up_factor.astype(jnp.float32)
    grad_hidden = scaled_sum(
        jnp.einsum("tkrc,krbc->tkrb", down_sel, down_blocks, preferred_element_type=jnp.float32),
        down_factor,
    )
    grad_down = lax.psum_scatter(
        (
            jnp.einsum("trb,tkrc->krbc", hidden, down_sel, preferred_element_type=jnp.float32)
            * down_float[:, :, None, None]
        ).astype(jnp.bfloat16),
        "fsdp",
        scatter_dimension=0,
        tiled=True,
    )
    grad_gate_act = (
        grad_hidden * up_pre * sigmoid_gate * (1.0 + gate_pre * (1.0 - sigmoid_gate))
    ).astype(jnp.bfloat16)
    grad_up_act = (grad_hidden * activated).astype(jnp.bfloat16)
    grad_gate = lax.psum_scatter(
        slot_term(gate_sel, grad_gate_act, gate_float).astype(jnp.bfloat16),
        "fsdp",
        scatter_dimension=0,
        tiled=True,
    )
    grad_up = lax.psum_scatter(
        slot_term(up_sel, grad_up_act, up_float).astype(jnp.bfloat16),
        "fsdp",
        scatter_dimension=0,
        tiled=True,
    )
    back_gate = (
        jnp.einsum("trb,krab->krta", grad_gate_act, gate_blocks, preferred_element_type=jnp.float32)
        * gate_float[:, :, None, None]
    )
    back_up = (
        jnp.einsum("trb,krab->krta", grad_up_act, up_blocks, preferred_element_type=jnp.float32)
        * up_float[:, :, None, None]
    )
    in_full = (
        jnp.zeros((nblocks, token_count, block_size), jnp.float32)
        .at[gate_where]
        .add(back_gate)
        .at[up_where]
        .add(back_up)
    )
    in_part = lax.psum_scatter(
        in_full.astype(jnp.bfloat16), "tensor", scatter_dimension=0, tiled=True
    ).astype(jnp.float32)
    grad_tokens = (
        jnp.transpose(in_part, (1, 0, 2))
        .reshape(token_count, local_blocks * block_size)
        .astype(jnp.bfloat16)
    )
    return (layer_out, grad_tokens, grad_gate, grad_up, grad_down)


def gather_kernel(shards, tokens, cotangent, *refs):
    rows, factors, (wg, wu, wd), refs = refs[:3], refs[3:6], refs[6:9], refs[9:]
    tok_all, rg, ru, rd, row_table, factor_table, spot, both, *sems = refs
    (z_send, z_recv, c_send, c_recv, x_send, x_recv, w_send, w_recv, y_send, y_recv, n_send, n_recv, s_send, s_recv, e_send, e_recv, here) = sems
    part, t, f = lax.axis_index("parts"), lax.axis_index("tensor"), lax.axis_index("fsdp")
    flip = [f, (f // 2) * 2 + 1 - f % 2, (f + 2) % 4, ((f + 2) % 4 // 2) * 2 + 1 - f % 2]
    count = rg.shape[2]
    last = shards - 1
    weights = ((wg, rg), (wu, ru), (wd, rd))

    def to(where, src, dst, send, recv):
        return pltpu.make_async_remote_copy(
            src_ref=src, dst_ref=dst, send_sem=send, recv_sem=recv,
            device_id=where, device_id_type=pl.DeviceIdType.MESH,
        )

    def across(m):
        return (part, t, flip[m])

    over = (1 - part, t, f)
    ups = ((part, t + 1, f), (part, t - 1, f))
    more = (t < last, t > 0)
    spot[0], spot[1] = f, t
    blk = both.shape[3]
    for which, ref in enumerate((tokens, cotangent)):
        for d in range(both.shape[1]):
            both[which, d] = ref[:, d * blk : (d + 1) * blk]
    for array in range(3):
        row_table[0, array] = rows[array][...]
        factor_table[0, array] = factors[array][...].astype(jnp.float32)

    barrier = pltpu.get_barrier_semaphore()
    for m in (1, 2, 3):
        pl.semaphore_signal(barrier, inc=1, device_id=across(m), device_id_type=pl.DeviceIdType.MESH)
    pl.semaphore_signal(barrier, inc=1, device_id=over, device_id_type=pl.DeviceIdType.MESH)
    for way in range(2):
        @pl.when(more[way])
        def _():
            pl.semaphore_signal(barrier, inc=1, device_id=ups[way], device_id_type=pl.DeviceIdType.MESH)
    ends = jnp.logical_or(t == 0, t == last)

    @pl.when(ends)
    def _():
        pl.semaphore_wait(barrier, 5)

    @pl.when(jnp.logical_not(ends))
    def _():
        pl.semaphore_wait(barrier, 6)

    def z_copy(way, src, x, own=False, hops=0):
        place = tok_all.at[0, src, x]
        if x == 1 and hops == last:
            place = tok_all.at[0, src, x, 0]
        return to(ups[way], both if own else place, place, z_send.at[way, src, x], z_recv.at[way, src, x])

    def e_copy(src):
        return to(across(2), tok_all.at[0, src, 0, 1], tok_all.at[0, src, 1, 1], e_send, e_recv)

    def c_copy(src, x, own=False):
        source = both if own else tok_all.at[0, src, x]
        return to(across(1), source, tok_all.at[1, src, x], c_send.at[src, x], c_recv.at[src, x])

    x_copy = to(across(2), both, tok_all.at[0, t, 1], x_send, x_recv)
    keep = pltpu.make_async_copy(both, tok_all.at[0, t, 0], here)
    x_copy.start()
    for way in range(2):
        @pl.when(more[way])
        def _():
            z_copy(way, t, 0, True).start()
    tables = [
        to(across(m), table.at[0], table.at[m], s_send.at[i, m - 1], s_recv.at[i, m - 1])
        for i, table in enumerate((row_table, factor_table))
        for m in (1, 2, 3)
    ]
    for c in tables:
        c.start()
    c_copy(t, 0, True).start()
    w_copies, y_copies, y_waits, n_copies = [], [], [], []
    for w, r in weights:
        for m in (2, 3):
            j = len(w_copies)
            w_copies.append(to(across(m), w.at[part, pl.ds(flip[m] * count, count)], r.at[m - 1, part], w_send.at[j], w_recv.at[j]))
            y_copies.append(to(over, r.at[m - 1, part], r.at[m - 1, part], y_send.at[j], y_recv.at[j]))
            y_waits.append(to(over, r.at[m - 1, part], r.at[m - 1, 1 - part], y_send.at[j], y_recv.at[j]))
        for k in range(2):
            j = len(n_copies)
            n_copies.append(to(across(1), w.at[k, pl.ds(flip[1] * count, count)], r.at[0, k], n_send.at[j], n_recv.at[j]))
    for c in w_copies:
        c.start()
    for c in n_copies:
        c.start()
    keep.start()

    x_copy.wait_recv()
    for way in range(2):
        @pl.when(more[way])
        def _():
            z_copy(way, t, 1, hops=1).start()
    c_copy(t, 1).start()

    def arrive(step, x):
        for way in range(2):
            src = t - step if way == 0 else t + step

            @pl.when(src >= 0 if way == 0 else src <= last)
            def _():
                z_copy(way, src, x, hops=step).wait_recv()

                @pl.when(more[way])
                def _():
                    z_copy(way, src, x, hops=step + 1).start()

                if step == last:
                    if x == 0:
                        e_copy(src).start()
                    else:
                        e_copy(src).wait_recv()

                c_copy(src, x).start()

    def relay(j):
        w_copies[j].wait_recv()
        y_copies[j].start()

    order = [(s, x) for s in range(1, shards) for x in range(2)]
    done = 0
    for i, (s, x) in enumerate(order):
        arrive(s, x)
        while done < len(w_copies) and done < 2 * i + 1:
            relay(done)
            done += 1
    while done < len(w_copies):
        relay(done)
        done += 1

    for way in range(2):
        for s in range(shards):
            src = t - s if way == 0 else t + s

            @pl.when(jnp.logical_and(src >= 0 if way == 0 else src <= last, more[way]))
            def _():
                for x in range(2):
                    z_copy(way, src, x, s == 0 and x == 0, s + 1).wait_send()

        @pl.when(t == last if way == 0 else t == 0)
        def _():
            e_copy(0 if way == 0 else last).wait_send()

    for src in range(shards):
        for x in range(2):
            c_copy(src, x).wait_send()
            c_copy(src, x).wait_recv()
    for c in tables + n_copies:
        c.wait_send()
        c.wait_recv()
    x_copy.wait_send()
    for c in w_copies + y_copies:
        c.wait_send()
    for c in y_waits:
        c.wait_recv()
    keep.wait()


def gather(tokens, cotangent, rows, factors, weights, shards):
    per_dev, local_cols, blk, _ = weights[0].shape
    count = local_cols // 4
    tok, width = tokens.shape
    bf = jnp.bfloat16
    dma = lambda *a: pltpu.SemaphoreType.DMA(a)
    received = jax.ShapeDtypeStruct((3, per_dev, count, blk, blk), bf)
    anywhere, local = pl.BlockSpec(memory_space=pl.ANY), pl.BlockSpec(memory_space=pltpu.VMEM)
    both = (2, width // blk, tok, blk)
    table = (4, 3, per_dev, local_cols)
    z = (2, shards, 2)
    c = (shards, 2)
    one = pltpu.SemaphoreType.DMA
    return pl.pallas_call(
        functools.partial(gather_kernel, shards),
        out_shape=[
            jax.ShapeDtypeStruct((2, shards, 2) + both, bf),
            received, received, received,
            jax.ShapeDtypeStruct(table, jnp.int32),
            jax.ShapeDtypeStruct(table, jnp.float32),
            jax.ShapeDtypeStruct((2,), jnp.int32),
        ],
        in_specs=[local] * 8 + [anywhere] * 3,
        out_specs=[anywhere] * 4 + [local] * 2 + [pl.BlockSpec(memory_space=pltpu.SMEM)],
        scratch_shapes=[
            pltpu.VMEM(both, bf),
            dma(*z), dma(*z), dma(*c), dma(*c), one, one, dma(6), dma(6), dma(6), dma(6), dma(6), dma(6), dma(2, 3), dma(2, 3), one, one, one,
        ],
        compiler_params=pltpu.CompilerParams(collective_id=0, has_side_effects=True),
    )(tokens, cotangent, *rows, *factors, *weights)


NN = (((1,), (0,)), ((), ()))
NT = (((1,), (1,)), ((), ()))
dot = functools.partial(lax.dot_general, preferred_element_type=jnp.float32)


def entry(table_ref, array, slot, r):
    per_dev = table_ref.shape[2]
    return table_ref[slot // per_dev, array, slot % per_dev, r]


def load(rows_ref, tok_ref, tok, which, array, slot, r, sel):
    per_shard, blk = tok_ref.shape[4], tok_ref.shape[6]
    place = entry(rows_ref, array, slot, r)
    shard, block = place // per_shard, place % per_shard
    for c in range(2):
        for x in range(2):
            q = c * 2 + x
            sel[q * tok : (q + 1) * tok, slot * blk : (slot + 1) * blk] = tok_ref[c, shard, x, which, block]


def scaled(scale_ref, own, recv, array, slot, r):
    per_dev = own.shape[0]
    src, sub = slot // per_dev, slot % per_dev
    value = recv[src - 1, sub, 0] if src else own[sub, 0]
    return (value.astype(jnp.float32) * entry(scale_ref, array, slot, r)).astype(jnp.bfloat16)


def accumulate(rows_ref, acc, array, slots, r, blk, product):
    for slot in range(slots):
        acc[entry(rows_ref, array, slot, r)] += product[:, slot * blk : (slot + 1) * blk]


def clear(acc):
    @pl.when(pl.program_id(0) == 0)
    def _():
        acc[...] = jnp.zeros_like(acc)


def flush(shard, acc, tok, own, other):
    per_shard = own[0].shape[1]

    @pl.when(pl.program_id(0) == pl.num_programs(0) - 1)
    def _():
        for m in range(len(own)):
            first = (shard ^ m) * per_shard
            for c, ref in enumerate((own[m], other[m])):
                for x in range(2):
                    q = c * 2 + x

                    @pl.loop(0, per_shard)
                    def _(d):
                        ref[x, d] = acc[first + d, q * tok : (q + 1) * tok, :].astype(jnp.bfloat16)


def early_kernel(dims, rows_ref, scale_ref, place_ref, tok_ref, *refs):
    slots, per_dev, tok, blk, shards = dims
    nsrc = slots // per_dev
    own_w, recv_w, refs = refs[:3], refs[3:6], refs[6:]
    grads, (gate_pre_ref, up_pre_ref), refs = refs[:nsrc], refs[nsrc : nsrc + 2], refs[nsrc + 2 :]
    own, other, scratch = refs[:shards], refs[shards : 2 * shards], refs[2 * shards :]
    acc, gate_sel, up_sel, down_sel, gate_w, up_w, down_w = scratch
    r = place_ref[0] * pl.num_programs(0) + pl.program_id(0)
    clear(acc)
    for slot in range(slots):
        span = slice(slot * blk, (slot + 1) * blk)
        load(rows_ref, tok_ref, tok, 0, 0, slot, r, gate_sel)
        load(rows_ref, tok_ref, tok, 0, 1, slot, r, up_sel)
        load(rows_ref, tok_ref, tok, 1, 2, slot, r, down_sel)
        gate_w[span, :] = scaled(scale_ref, own_w[0], recv_w[0], 0, slot, r)
        up_w[span, :] = scaled(scale_ref, own_w[1], recv_w[1], 1, slot, r)
        down_w[:, span] = scaled(scale_ref, own_w[2], recv_w[2], 2, slot, r)
    gate_pre = dot(gate_sel[...], gate_w[...], NN)
    up_pre = dot(up_sel[...], up_w[...], NN)
    gate_pre_ref[0], up_pre_ref[0] = gate_pre, up_pre
    hidden = (gate_pre * jax.nn.sigmoid(gate_pre) * up_pre).astype(jnp.bfloat16)
    down = dot(hidden.T, down_sel[...], NN)
    for slot in range(slots):
        src, sub = slot // per_dev, slot % per_dev
        g = down[:, slot * blk : (slot + 1) * blk] * entry(scale_ref, 2, slot, r)
        grads[src][sub, 0] = g.astype(jnp.bfloat16)
    accumulate(rows_ref, acc, 2, slots, r, blk, dot(hidden, down_w[...], NN))
    flush(place_ref[1], acc, tok, own, other)


def middle_kernel(dims, rows_ref, scale_ref, place_ref, tok_ref, own_w, recv_w, gate_pre_ref, up_pre_ref, *refs):
    slots, per_dev, tok, blk, _ = dims
    nsrc = slots // per_dev
    grads, (gate_act_ref, up_act_ref), scratch = (refs[:nsrc], refs[nsrc : 2 * nsrc]), refs[2 * nsrc : 2 * nsrc + 2], refs[2 * nsrc + 2 :]
    gate_sel, up_sel, down_sel, down_w = scratch
    r = place_ref[0] * pl.num_programs(0) + pl.program_id(0)
    for slot in range(slots):
        load(rows_ref, tok_ref, tok, 0, 0, slot, r, gate_sel)
        load(rows_ref, tok_ref, tok, 0, 1, slot, r, up_sel)
        load(rows_ref, tok_ref, tok, 1, 2, slot, r, down_sel)
        down_w[:, slot * blk : (slot + 1) * blk] = scaled(scale_ref, own_w, recv_w, 2, slot, r)
    gate_pre, up_pre = gate_pre_ref[0], up_pre_ref[0]
    grad_hidden = dot(down_sel[...], down_w[...], NT)
    sig = jax.nn.sigmoid(gate_pre)
    act = gate_pre * sig
    gate_act = (grad_hidden * up_pre * sig * (1.0 + gate_pre * (1.0 - sig))).astype(jnp.bfloat16)
    up_act = (grad_hidden * act).astype(jnp.bfloat16)
    gate_act_ref[0], up_act_ref[0] = gate_act, up_act
    for array, (sel, act) in enumerate(((gate_sel, gate_act), (up_sel, up_act))):
        product = dot(act.T, sel[...], NN)
        for slot in range(slots):
            src, sub = slot // per_dev, slot % per_dev
            g = product[:, slot * blk : (slot + 1) * blk] * entry(scale_ref, array, slot, r)
            grads[array][src][sub, 0] = g.astype(jnp.bfloat16).T


def late_kernel(dims, rows_ref, scale_ref, place_ref, *refs):
    slots, per_dev, tok, blk, shards = dims
    nsrc = slots // per_dev
    own_w, recv_w, (gate_act_ref, up_act_ref), pieces, refs = refs[:2], refs[2:4], refs[4:6], refs[6 : 6 + nsrc], refs[6 + nsrc :]
    own_ref, other_ref, placed_ref, acc, gate_w, up_w = refs
    own, other = [own_ref.at[d] for d in range(shards)], [other_ref.at[d] for d in range(shards)]
    r = place_ref[0] * pl.num_programs(0) + pl.program_id(0)
    clear(acc)
    for m, piece in enumerate(pieces):
        placed_ref[:, place_ref[0] ^ m, 0] = piece[:, 0]
    for slot in range(slots):
        span = slice(slot * blk, (slot + 1) * blk)
        gate_w[span, :] = scaled(scale_ref, own_w[0], recv_w[0], 0, slot, r)
        up_w[span, :] = scaled(scale_ref, own_w[1], recv_w[1], 1, slot, r)
    accumulate(rows_ref, acc, 0, slots, r, blk, dot(gate_act_ref[0], gate_w[...], NT))
    accumulate(rows_ref, acc, 1, slots, r, blk, dot(up_act_ref[0], up_w[...], NT))
    flush(0, acc, tok, own, other)


def columns(which, scalars, tok_all, own_w, recv_w, kept):
    nsrc = 1 + recv_w[0].shape[0]
    _, per_dev, count, blk, _ = recv_w[0].shape
    _, shards, _, _, per_shard, tok, _ = tok_all.shape
    nblk = shards * per_shard
    slots = per_dev * nsrc
    total = 4 * tok
    bf, f32 = jnp.bfloat16, jnp.float32
    whole = lambda a: pl.BlockSpec(a, lambda r, *_: (0,) * len(a), pipeline_mode=pl.Buffered(1))
    own_block = pl.BlockSpec((per_dev, 1, blk, blk), lambda r, rows, scale, at: (0, at[0] * count + r, 0, 0))
    recv_block = pl.BlockSpec((nsrc - 1, per_dev, 1, blk, blk), lambda r, *_: (0, 0, r, 0, 0))
    block = pl.BlockSpec((per_dev, 1, blk, blk), lambda r, *_: (0, r, 0, 0))
    piece = jax.ShapeDtypeStruct((per_dev, count, blk, blk), bf)
    kept_block = [pl.BlockSpec((1, total, blk), lambda r, *_: (r, 0, 0))] * 2
    keep = lambda kind: [jax.ShapeDtypeStruct((count, total, blk), kind)] * 2
    share = (2, per_shard, tok, blk)
    acc = pltpu.VMEM((nblk, total, blk), f32)
    sel = pltpu.VMEM((total, slots * blk), bf)
    tall, wide = pltpu.VMEM((slots * blk, blk), bf), pltpu.VMEM((blk, slots * blk), bf)
    dims = (slots, per_dev, tok, blk, shards)
    if which == "early":
        body, products = functools.partial(early_kernel, dims), 4
        in_specs = [whole(tok_all.shape)] + [own_block] * 3 + [recv_block] * 3
        operands = (tok_all, *own_w, *recv_w)
        out_specs = [block] * nsrc + kept_block + [whole(share)] * (2 * shards)
        out_shape = [piece] * nsrc + keep(f32) + [jax.ShapeDtypeStruct(share, bf)] * (2 * shards)
        scratch = [acc, sel, sel, sel, tall, tall, wide]
    elif which == "late":
        body, products = functools.partial(late_kernel, dims), 2
        in_specs = [own_block] * 2 + [recv_block] * 2 + kept_block + [block] * nsrc
        operands = (*own_w[:2], *recv_w[:2], *kept)
        placed = pl.BlockSpec((per_dev, nsrc, 1, blk, blk), lambda r, *_: (0, 0, r, 0, 0))
        out_specs = [whole((shards,) + share)] * 2 + [placed]
        out_shape = [jax.ShapeDtypeStruct((shards,) + share, bf)] * 2
        out_shape += [jax.ShapeDtypeStruct((per_dev, nsrc, count, blk, blk), bf)]
        scratch = [acc, tall, tall]
    else:
        body, products = functools.partial(middle_kernel, dims), 3
        in_specs = [whole(tok_all.shape), own_block, recv_block] + kept_block
        operands = (tok_all, own_w[2], recv_w[2], *kept)
        out_specs, out_shape = [block] * (2 * nsrc) + kept_block, [piece] * (2 * nsrc) + keep(bf)
        scratch = [sel, sel, sel, wide]
    flops = 2 * products * slots * count * total * blk * blk
    return pl.pallas_call(
        body,
        grid_spec=pltpu.PrefetchScalarGridSpec(
            num_scalar_prefetch=3, grid=(count,), in_specs=in_specs, out_specs=out_specs, scratch_shapes=scratch,
        ),
        out_shape=out_shape,
        compiler_params=pltpu.CompilerParams(vmem_limit_bytes=64_600_000 if which == "late" else 60 * 1024 * 1024),
        cost_estimate=pl.CostEstimate(flops=flops, bytes_accessed=40 << 20, transcendentals=0),
    )(*scalars, *operands)


def add_kernel(pairs, *refs):
    left, right, out, (held, load_sem, store_sem) = refs[:pairs], refs[pairs : 2 * pairs], refs[2 * pairs : 3 * pairs], refs[3 * pairs :]
    loads = [[pltpu.make_async_copy(a, held.at[i, m], load_sem.at[i, m]) for m, a in enumerate(side)] for i, side in enumerate((left, right))]
    stores = [pltpu.make_async_copy(held.at[2, m], c, store_sem.at[m]) for m, c in enumerate(out)]
    for m in reversed(range(pairs)):
        loads[0][m].start()
        loads[1][m].start()
    for m in reversed(range(pairs)):
        loads[0][m].wait()
        loads[1][m].wait()
        held[2, m] = (held[0, m].astype(jnp.float32) + held[1, m].astype(jnp.float32)).astype(held.dtype)
        stores[m].start()
    for c in stores:
        c.wait()


def add_pairs(left, right):
    pairs, unit = len(left), left[0]
    anywhere, dma = pl.BlockSpec(memory_space=pl.ANY), pltpu.SemaphoreType.DMA
    return pl.pallas_call(
        functools.partial(add_kernel, pairs),
        in_specs=[anywhere] * (2 * pairs),
        out_specs=[anywhere] * pairs,
        out_shape=[jax.ShapeDtypeStruct(unit.shape, unit.dtype)] * pairs,
        scratch_shapes=[pltpu.VMEM((3, pairs) + unit.shape, unit.dtype), dma((2, pairs)), dma((pairs,))],
        compiler_params=pltpu.CompilerParams(vmem_limit_bytes=66_400_000),
    )(*left, *right)


def reduce_kernel(shards, own, other, first, *refs):
    shares, refs = refs[: shards - 1], refs[shards - 1 :]
    (out_ref, in_ref, chip, core_box, line_box, far, far_box, near, early,
     load_sem, core_send, core_recv, line_send, line_recv, far_send, far_recv, early_sem) = refs
    part, t, f = lax.axis_index("parts"), lax.axis_index("tensor"), lax.axis_index("fsdp")
    last = shards - 1
    f32, bf = jnp.float32, jnp.bfloat16
    partner = (part, t, (f // 2) * 2 + 1 - f % 2)
    across = (part, t, (f + 2) % 4)

    def to(where, src, dst, send, recv):
        return pltpu.make_async_remote_copy(
            src_ref=src, dst_ref=dst, send_sem=send, recv_sem=recv,
            device_id=where, device_id_type=pl.DeviceIdType.MESH,
        )

    barrier = pltpu.get_barrier_semaphore()
    for where in (partner, across):
        pl.semaphore_signal(barrier, inc=1, device_id=where, device_id_type=pl.DeviceIdType.MESH)

    @pl.when(t > 0)
    def _():
        pl.semaphore_signal(barrier, inc=1, device_id=(part, t - 1, f), device_id_type=pl.DeviceIdType.MESH)

    @pl.when(t < last)
    def _():
        pl.semaphore_signal(barrier, inc=1, device_id=(part, t + 1, f), device_id_type=pl.DeviceIdType.MESH)

    ends = jnp.logical_or(t == 0, t == last)

    @pl.when(ends)
    def _():
        pl.semaphore_wait(barrier, 3)

    @pl.when(jnp.logical_not(ends))
    def _():
        pl.semaphore_wait(barrier, 4)

    def place(i):
        return jnp.where(t * 2 < shards, last - i, i)

    order = [(i, x) for i in range(shards) for x in (1, 0)]
    cores, loads = {}, {}
    for i, x in order:
        d = place(i)
        cores[i, x] = to(partner, other.at[d, x], core_box.at[d, x], core_send.at[d, x], core_recv.at[d, x])
        loads[i, x] = pltpu.make_async_copy(own.at[d, x], chip.at[d, x], load_sem.at[d, x])
        cores[i, x].start()
        loads[i, x].start()
    fetch = [
        pltpu.make_async_copy(ref, early.at[k], early_sem.at[k]) for k, ref in enumerate((first,) + tuple(shares))
    ]
    for c in fetch:
        c.start()

    def line(up, d, x):
        where = (part, jnp.where(up, t + 1, t - 1), f)
        w = jnp.where(up, 0, 1)
        return to(where, chip.at[d, x], line_box.at[w, d, x], line_send.at[w, d, x], line_recv.at[w, d, x])

    def gathered(i, x):
        d = place(i)
        loads[i, x].wait()
        cores[i, x].wait_recv()
        chip[d, x] = (chip[d, x].astype(f32) + core_box[d, x].astype(f32)).astype(bf)

    def forward(up, i, x):
        d = jnp.where(up, last - i, i)
        w = jnp.where(up, 0, 1)
        fed = jnp.where(up, t > 0, t < last)

        @pl.when(jnp.where(up, t < d, t > d))
        def _():
            @pl.when(fed)
            def _():
                line(up, d, x).wait_recv()
                chip[d, x] = (chip[d, x].astype(f32) + line_box[w, d, x].astype(f32)).astype(bf)

            line(up, d, x).start()

    low = t * 2 < shards
    for i, x in order:
        gathered(i, x)

        @pl.when(jnp.where(low, t == 0, t == last))
        def _():
            forward(low, i, x)

    for i in range(shards - 1):
        for x in (1, 0):
            @pl.when(jnp.logical_not(ends))
            def _():
                forward(low, i, x)

        for x in (1, 0):
            forward(jnp.logical_not(low), i, x)

    def send_far(k):
        return to(across, far.at[k], far_box.at[k], far_send.at[k], far_recv.at[k])

    for c in fetch:
        c.wait()

    def early_sum(x):
        return sum(early[k, x].astype(f32) for k in range(shards))

    far[0] = early_sum(1).astype(bf)
    send_far(0).start()
    near[0] = early_sum(0)

    def late_sum(x):
        near[1] = chip[t, x].astype(f32)
        for up in (True, False):
            @pl.when(t > 0 if up else t < last)
            def _():
                line(jnp.bool_(up), t, x).wait_recv()
                near[1] += line_box[0 if up else 1, t, x].astype(f32)

    late_sum(1)
    far[1] = near[1].astype(bf)
    send_far(1).start()
    late_sum(0)
    blocks, blk = near.shape[1], near.shape[3]
    for k, ref in enumerate((out_ref, in_ref)):
        send_far(k).wait_recv()
        for d in range(blocks):
            ref[:, d * blk : (d + 1) * blk] = (near[k, d] + far_box[k, d].astype(f32)).astype(bf)
    for k in range(2):
        send_far(k).wait_send()
    for i, x in order:
        cores[i, x].wait_send()
    for d in range(shards):
        for x in range(2):
            @pl.when(t < d)
            def _():
                line(jnp.bool_(True), d, x).wait_send()

            @pl.when(t > d)
            def _():
                line(jnp.bool_(False), d, x).wait_send()


def reduce(own, other, shares, width):
    shards, _, blocks, tok, blk = own.shape
    bf, f32 = jnp.bfloat16, jnp.float32
    dma = lambda *a: pltpu.SemaphoreType.DMA(a)
    anywhere = pl.BlockSpec(memory_space=pl.ANY)
    unit = (blocks, tok, blk)
    pair = (shards, 2)
    return pl.pallas_call(
        functools.partial(reduce_kernel, shards),
        out_shape=[jax.ShapeDtypeStruct((tok, width), bf)] * 2,
        in_specs=[anywhere] * (2 + shards),
        out_specs=[pl.BlockSpec(memory_space=pltpu.VMEM)] * 2,
        scratch_shapes=[
            pltpu.VMEM(pair + unit, bf), pltpu.VMEM(pair + unit, bf), pltpu.VMEM((2,) + pair + unit, bf),
            pltpu.VMEM((2,) + unit, bf), pltpu.VMEM((2,) + unit, bf), pltpu.VMEM((2,) + unit, f32),
            pltpu.VMEM(pair + unit, bf),
            dma(*pair), dma(*pair), dma(*pair), dma(2, *pair), dma(2, *pair), dma(2), dma(2), dma(shards),
        ],
        compiler_params=pltpu.CompilerParams(collective_id=1, has_side_effects=True, vmem_limit_bytes=66_400_000),
    )(own, other, *shares)


def home_kernel(arrays, place_ref, *refs):
    nsrc = (len(refs) - 3) // arrays - 1
    pieces, placed, (held, load_sem, store_sem) = refs[: arrays * nsrc], refs[arrays * nsrc : -3], refs[-3:]
    count = held.shape[2]
    loads, stores = [], []
    for j, piece in enumerate(pieces):
        array, m = j // nsrc, j % nsrc
        for sub in range(piece.shape[0]):
            column = (place_ref[0] ^ m) * count
            loads.append(pltpu.make_async_copy(piece.at[sub], held.at[j, sub], load_sem.at[j, sub]))
            stores.append(
                pltpu.make_async_copy(held.at[j, sub], placed[array].at[sub, pl.ds(column, count)], store_sem.at[j, sub])
            )
    for c in loads:
        c.start()
    for a, b in zip(loads, stores):
        a.wait()
        b.start()
    for c in stores:
        c.wait()


def home(place, sent):
    arrays, nsrc = len(sent), len(sent[0])
    per_dev, count, blk, _ = sent[0][0].shape
    anywhere = pl.BlockSpec(memory_space=pl.ANY)
    shape = jax.ShapeDtypeStruct((per_dev, nsrc * count, blk, blk), sent[0][0].dtype)
    held = (arrays * nsrc, per_dev)
    return pl.pallas_call(
        functools.partial(home_kernel, arrays),
        grid_spec=pltpu.PrefetchScalarGridSpec(
            num_scalar_prefetch=1, grid=(1,),
            in_specs=[anywhere] * (arrays * nsrc), out_specs=[anywhere] * arrays,
            scratch_shapes=[
                pltpu.VMEM(held + (count, blk, blk), sent[0][0].dtype), pltpu.SemaphoreType.DMA(held), pltpu.SemaphoreType.DMA(held),
            ],
        ),
        out_shape=[shape] * arrays,
        compiler_params=pltpu.CompilerParams(vmem_limit_bytes=66_400_000),
    )(place, *[piece for pieces in sent for piece in pieces])


def swap(value, flip, axis="fsdp"):
    return lax.ppermute(value, axis, [(i, i ^ flip) for i in range(lax.axis_size(axis))])


def exchanged_plan(
    tokens,
    cotangent,
    gate_values,
    gate_rows,
    gate_scale,
    up_values,
    up_rows,
    up_scale,
    down_values,
    down_cols,
    down_scale,
):
    _, width = tokens.shape
    shards = lax.axis_size("tensor")
    own_w = (gate_values, up_values, down_values)
    rows, factors = (gate_rows, up_rows, down_cols), (gate_scale, up_scale, down_scale)
    tok_all, *recv_w, row_table, factor_table, place = gather(tokens, cotangent, rows, factors, own_w, shards)
    scalars = (row_table, factor_table, place)

    def send(pieces):
        return [p if m == 0 else swap(p, m) for m, p in enumerate(pieces)]

    early = columns("early", scalars, tok_all, own_w, recv_w, ())
    down_pieces, pre, own, other = early[:4], early[4:6], early[6 : 6 + shards], early[6 + shards :]
    chip = add_pairs(own, [swap(b, 1) for b in other])
    down_sent = send(down_pieces)
    chip, pre = lax.optimization_barrier((chip, pre))
    out_shares = [c if m == 0 else swap(c, m, "tensor") for m, c in enumerate(chip)]
    middle = columns("middle", scalars, tok_all, own_w, recv_w, pre)
    gate_sent, up_sent = send(middle[:4]), send(middle[4:8])
    own, other, grad_down = columns("late", scalars, tok_all, own_w, recv_w, (*middle[8:], *down_sent))
    layer_out, grad_tokens = reduce(own, other, out_shares, width)
    grad_gate, grad_up = home(place, (gate_sent, up_sent))
    return (layer_out, grad_tokens, grad_gate, grad_up, grad_down.reshape(gate_values.shape))


def choose_plan(mesh, *args):
    fits = mesh.shape["fsdp"] == 4 and mesh.shape["parts"] == 2 and args[2].shape[0] == 2
    fits = fits and args[2].shape[1] % 4 == 0 and mesh.shape["tensor"] in (2, 4, 8)
    plan = exchanged_plan if fits else gathered_plan
    return plan(*args)


def solution(mesh):
    plan = functools.partial(choose_plan, mesh)
    in_specs = (
        P(("parts", "fsdp"), "tensor"),
        P(("parts", "fsdp"), "tensor"),
        P("fsdp", "tensor", None, None),
        P("fsdp", "tensor"),
        P("fsdp", "tensor"),
        P("fsdp", "tensor", None, None),
        P("fsdp", "tensor"),
        P("fsdp", "tensor"),
        P("fsdp", "tensor", None, None),
        P("fsdp", "tensor"),
        P("fsdp", "tensor"),
    )
    out_specs = (
        P(("parts", "fsdp"), "tensor"),
        P(("parts", "fsdp"), "tensor"),
        P(("parts", "fsdp"), "tensor", None, None),
        P(("parts", "fsdp"), "tensor", None, None),
        P(("parts", "fsdp"), "tensor", None, None),
    )
    return jax.shard_map(plan, mesh=mesh, in_specs=in_specs, out_specs=out_specs, check_vma=False)
```
